512 devices in a mesh: row: 32 (over z_hi, y, core), col: 16 (over x, z_lo).
Axes of the slice: x: 4, y: 8, z: 8 (z_hi: 2, z_lo: 4; z = z_hi * 4 + z_lo), core: 2. Of those that a mesh axis runs over, the one named last changes fastest.
Arguments:
- object_re: float32 [12288, 8192], P('row', 'col'), may hold values from -6 to 6
- object_im: float32 [12288, 8192], P('row', 'col'), may hold values from -6 to 6
- probe_re: float32 [256, 256], replicated, may hold values from -6 to 6
- probe_im: float32 [256, 256], replicated, may hold values from -6 to 6
- frames: bfloat16 [32, 16, 8, 256, 256], P('row', 'col'), may hold values from 0.049804688 to 20
- counts: int32 [32, 16], P('row', 'col'), may hold values from 1 to 8, as said below
- offsets: int32 [32, 16, 8, 2], P('row', 'col'), may hold values from -32 to 288, as said below
- frame_index: int32 [32, 16, 8], P('row', 'col'), may hold values from 0 to 7
Outputs:
- new_re: float32 [12288, 8192], P('row', 'col')
- new_im: float32 [12288, 8192], P('row', 'col')
The draws below stay inside these ranges and needn't reach their ends.
Inputs may be any that keep to these rules, and one draw needn't show every extreme that they name: `counts`: in every draw some tile has 8 positions and some tile has one. Row offsets are -32 plus multiples of 16, at most 160; column offsets likewise, at most 288; in every draw some live position has both offsets at the lowest value and some has both at the highest.
All inputs are finite; a program needn't handle non-finite values.
Results may differ from the reference program's by a relative error of at most 0.0003.
Values sent between devices are 32-bit elements; how exact they have to be, the bound alone decides.
A program may use at most 64 MiB of HBM per device.

```python
import math
import jax
import jax.numpy as jnp
from jax import lax

TILE_R = 384
TILE_C = 512
P_SIZE = 256
HALO = 32
STEP = 16
MAXPOS = 8
FRAMES = 8
NR = 12288
NC = 8192
N_ROW = 32
N_COL = 16


def draw_counts(key, part):
    first_key, second_key, high_key, low_key = jax.random.split(jax.random.fold_in(key, 11), 4)
    first = jax.random.randint(first_key, (N_ROW * N_COL,), 0, MAXPOS)
    second = jax.random.randint(second_key, (N_ROW * N_COL,), 0, MAXPOS)
    counts = 1 + first * second // (MAXPOS - 1)
    high_spot = jax.random.randint(high_key, (), 0, N_ROW * N_COL)
    low_spot = (high_spot + 1 + jax.random.randint(low_key, (), 0, N_ROW * N_COL - 1)) % (N_ROW * N_COL)
    counts = counts.at[high_spot].set(MAXPOS).at[low_spot].set(1)
    return counts.reshape(N_ROW, N_COL).astype(jnp.int32)


def draw_offsets(key, part):
    row_key, col_key, low_key, high_key = jax.random.split(jax.random.fold_in(key, 23), 4)
    row_steps = (TILE_R - P_SIZE + 2 * HALO) // STEP + 1
    col_steps = (TILE_C - P_SIZE + 2 * HALO) // STEP + 1
    rows = -HALO + STEP * jax.random.randint(row_key, (N_ROW * N_COL, MAXPOS), 0, row_steps)
    cols = -HALO + STEP * jax.random.randint(col_key, (N_ROW * N_COL, MAXPOS), 0, col_steps)
    low_spot = jax.random.randint(low_key, (), 0, N_ROW * N_COL)
    high_spot = (low_spot + 1 + jax.random.randint(high_key, (), 0, N_ROW * N_COL - 1)) % (N_ROW * N_COL)
    rows = rows.at[low_spot, 0].set(-HALO).at[high_spot, 0].set(TILE_R - P_SIZE + HALO)
    cols = cols.at[low_spot, 0].set(-HALO).at[high_spot, 0].set(TILE_C - P_SIZE + HALO)
    both = jnp.stack([rows, cols], axis=-1)
    return both.reshape(N_ROW, N_COL, MAXPOS, 2).astype(jnp.int32)


def place_ends(values, own_key, smallest, largest):
    extent = values.shape
    index_at = [jax.random.randint(jax.random.fold_in(own_key, axis), (), 0, extent[axis]) for axis in range(len(extent))]
    values = values.at[tuple(index_at)].set(smallest)
    longest = extent.index(max(extent))
    index_at[longest] = (index_at[longest] + 1) % extent[longest]
    return values.at[tuple(index_at)].set(largest)


def block_levels(stream_key, shape, shards, low, high):
    level = 1.0
    for dim, parts in shards:
        steps = jax.random.uniform(jax.random.fold_in(jax.random.fold_in(stream_key, 6), dim), (parts,), jnp.float32, low / len(shards), high / len(shards))
        level = level * jnp.repeat(jnp.exp(steps), shape[dim] // parts).reshape((-1,) + (1,) * (len(shape) - 1 - dim))
    return level


def normal_values(stream_key, shape, spread, limit, cuts=(), kind=jnp.bfloat16):
    factor_of = block_levels(stream_key, shape, cuts, -0.22, 0.18) if cuts else 1.0
    drawn = jax.random.normal(stream_key, shape, jnp.float32) * spread * factor_of
    return jnp.minimum(jnp.maximum(drawn, -limit), limit).astype(kind)


def setup_inputs(seed: int = 0) -> dict:
    seeds = jax.random.split(jax.random.key(seed), 9)
    object_re = normal_values(seeds[0], (NR, NC), 1.0, 6.0, ((0, 32), (1, 16)), jnp.float32)
    object_im = normal_values(seeds[1], (NR, NC), 1.0, 6.0, ((0, 32), (1, 16)), jnp.float32)
    probe_re = normal_values(seeds[2], (P_SIZE, P_SIZE), 1.0, 6.0, (), jnp.float32)
    probe_im = normal_values(seeds[3], (P_SIZE, P_SIZE), 1.0, 6.0, (), jnp.float32)
    frames = jnp.clip(jnp.exp(math.log(20.0) - 5.9953784 * jax.random.uniform(seeds[4], (N_ROW, N_COL, FRAMES, P_SIZE, P_SIZE), jnp.float32) ** block_levels(seeds[4], (N_ROW, N_COL, FRAMES, P_SIZE, P_SIZE), ((0, 32), (1, 16)), -0.2, 0.2)), 0.049804688, 20.0).astype(jnp.bfloat16)
    counts = draw_counts(jax.random.fold_in(seeds[8], 71), 0)
    offsets = draw_offsets(jax.random.fold_in(seeds[8], 71), 0)
    frame_index = place_ends(jax.random.randint(seeds[7], (N_ROW, N_COL, MAXPOS), 0, FRAMES), jax.random.fold_in(seeds[7], 1), 0, FRAMES - 1).astype(jnp.int32)
    return dict(object_re=object_re, object_im=object_im, probe_re=probe_re, probe_im=probe_im, frames=frames, counts=counts, offsets=offsets, frame_index=frame_index)


floor_amp = 0.5
ridge = 1.0

def slot_gradient(patch_re, patch_im, probe, frame):
    patch = lax.complex(patch_re, patch_im)
    far = jnp.fft.fft2(probe * patch, norm='ortho')
    amplitude = jnp.abs(far)
    factor = 1.0 - jnp.sqrt(frame) / jnp.maximum(amplitude, floor_amp)
    back = jnp.fft.ifft2(far * factor, norm='ortho')
    grad = jnp.conj(probe) * back
    return (jnp.real(grad), jnp.imag(grad))

def reference(object_re, object_im, probe_re, probe_im, frames, counts, offsets, frame_index):
    pad_re = jnp.pad(object_re, HALO)
    pad_im = jnp.pad(object_im, HALO)
    probe = lax.complex(probe_re, probe_im)
    power = probe_re * probe_re + probe_im * probe_im
    zeros = jnp.zeros((3,) + pad_re.shape, object_re.dtype)

    def visit(acc, item):
        tile = item // MAXPOS
        slot = item % MAXPOS
        trow = tile // N_COL
        tcol = tile % N_COL
        live = (slot < counts[trow, tcol]).astype(object_re.dtype)
        row_start = (trow * TILE_R + offsets[trow, tcol, slot, 0] + HALO).astype(jnp.int32)
        col_start = (tcol * TILE_C + offsets[trow, tcol, slot, 1] + HALO).astype(jnp.int32)
        patch_re = lax.dynamic_slice(pad_re, (row_start, col_start), (P_SIZE, P_SIZE))
        patch_im = lax.dynamic_slice(pad_im, (row_start, col_start), (P_SIZE, P_SIZE))
        frame = frames[trow, tcol, frame_index[trow, tcol, slot]].astype(object_re.dtype)
        grad_re, grad_im = slot_gradient(patch_re, patch_im, probe, frame)
        term = jnp.stack([grad_re, grad_im, power]) * live
        start = (jnp.int32(0), row_start, col_start)
        acc = lax.dynamic_update_slice(acc, lax.dynamic_slice(acc, start, (3, P_SIZE, P_SIZE)) + term, start)
        return (acc, None)
    acc, _ = lax.scan(visit, zeros, jnp.arange(N_ROW * N_COL * MAXPOS, dtype=jnp.int32))
    inner = acc[:, HALO:HALO + NR, HALO:HALO + NC]
    denom = inner[2] + ridge
    return (object_re - inner[0] / denom, object_im - inner[1] / denom)
```

```python
import math

import jax
import jax.numpy as jnp
import numpy as np
from jax import lax
from jax.experimental import pallas as pl
from jax.experimental.pallas import tpu as pltpu
from jax.sharding import PartitionSpec as P

HALO = 32
F32, BF16 = jnp.float32, jnp.bfloat16
ridge = 1.0


def padded_2(cells, sides, width):
    for axis, dim in sides:
        count = lax.axis_size(axis)
        ends = count - 1
        head = lax.slice_in_dim(cells, 0, width, axis=dim)
        tail = lax.slice_in_dim(cells, cells.shape[dim] - width, cells.shape[dim], axis=dim)
        cells = jnp.concatenate(
            [
                lax.ppermute(tail, axis, [(i, (i + 1) % count) for i in range(ends)]),
                cells,
                lax.ppermute(head, axis, [((i + 1) % count, i) for i in range(ends)]),
            ],
            axis=dim,
        )
    return cells


def passed_along(shard, axis, by):
    devices = lax.axis_size(axis)
    pairs = [(i, i + by) for i in range(devices) if 0 <= i + by < devices]
    return lax.ppermute(shard, axis, pairs)


def tables():
    n = np.arange(128)[:, None]
    k = np.arange(128)[None, :]
    out = []
    for angle in (2 * np.pi * (n * k % 128) / 128, 2 * np.pi * (n * (2 * k + 1) % 256) / 256):
        c, s = np.cos(angle) / 16, np.sin(angle) / 16
        m = np.block([[c, -s], [s, c]])
        out += [m, m.T]
    full = np.stack(out)
    hi = full.astype(np.float32).astype(BF16)
    lo = (full - hi.astype(np.float64)).astype(np.float32).astype(BF16)
    return np.stack([hi, lo], axis=1)

def split(x):
    hi = x.astype(BF16)
    lo = (x - hi.astype(F32)).astype(BF16)
    return hi, lo

def right(x, tab, t):
    hi, lo = split(x)
    th, tl = tab[t, 0], tab[t, 1]
    return jnp.dot(jnp.concatenate([hi, lo, hi], 1), jnp.concatenate([th, th, tl], 0), preferred_element_type=F32)

def left(x, tab, t):
    hi, lo = split(x)
    th, tl = tab[t, 0], tab[t, 1]
    return jnp.dot(jnp.concatenate([th, th, tl], 1), jnp.concatenate([hi, lo, hi], 0), preferred_element_type=F32)

def slot_terms(blocks, wr, wi, amp, tab):
    e_re = [wr[b] * blocks(0, b) - wi[b] * blocks(1, b) for b in (0, 1)]
    e_im = [wr[b] * blocks(1, b) + wi[b] * blocks(0, b) for b in (0, 1)]
    even = right(jnp.concatenate([e_re[0] + e_re[1], e_im[0] + e_im[1]], 1), tab, 0)
    odd = right(jnp.concatenate([e_re[0] - e_re[1], e_im[0] - e_im[1]], 1), tab, 2)
    def halves(op):
        a, b = op(even[:128], even[128:]), op(odd[:128], odd[128:])
        return jnp.concatenate([jnp.concatenate([a[:, :128], b[:, :128]], 1), jnp.concatenate([a[:, 128:], b[:, 128:]], 1)], 0)
    u = left(halves(lambda p, q: p + q), tab, 1)
    v = left(halves(lambda p, q: p - q), tab, 3)
    def scaled(f, a):
        re, im = f[:128], f[128:]
        factor = 1.0 - a * lax.rsqrt(jnp.maximum(re * re + im * im, 0.25))
        return jnp.concatenate([re * factor, im * factor], 0)
    a = left(scaled(u, amp[:128]), tab, 0)
    b = left(scaled(v, amp[128:]), tab, 2)
    top, bot = a + b, a - b
    re = jnp.concatenate([top[:128], bot[:128]], 0)
    im = jnp.concatenate([top[128:], bot[128:]], 0)
    a = right(jnp.concatenate([re[:, :128], im[:, :128]], 1), tab, 1)
    b = right(jnp.concatenate([re[:, 128:], im[:, 128:]], 1), tab, 3)
    back = (a + b, a - b)
    t_re = [wr[i] * back[i][:, :128] + wi[i] * back[i][:, 128:] for i in (0, 1)]
    t_im = [wr[i] * back[i][:, 128:] - wi[i] * back[i][:, :128] for i in (0, 1)]
    return t_re, t_im

def permuted_amp(frame):
    r = lax.broadcasted_iota(jnp.int32, (256, 256), 0)
    c = lax.broadcasted_iota(jnp.int32, (256, 256), 1)
    def perm(j):
        return jnp.where(j < 128, 2 * j, 2 * j - 255)
    pc = (r == perm(c)).astype(F32).astype(BF16)
    pr = (c == perm(r)).astype(F32).astype(BF16)
    mixed = jnp.dot(frame, pc, preferred_element_type=F32).astype(BF16)
    return jnp.sqrt(jnp.dot(pr, mixed, preferred_element_type=F32))

def lanes(rows=256):
    return lax.broadcasted_iota(jnp.int32, (rows, 128), 1)

def kernel(count_ref, off_ref, idx_ref, po_ref, frames_ref, wr_ref, wi_ref, tab_ref, acc_ref, light_ref):
    acc_ref[...] = jnp.zeros_like(acc_ref)
    light_ref[...] = jnp.zeros_like(light_ref)
    def step(s, _):
        p = pl.multiple_of(off_ref[2 * s] + 32, 16)
        c = off_ref[2 * s + 1]
        rows = pl.ds(p, 256)
        lane = lanes()
        cm = lax.rem(c + 256, 256)
        sh = lax.rem(cm, 128)
        swap = cm // 128
        m = (1 - 2 * swap) * (lane - sh) - swap < 0
        def rolled(ref):
            a, b = (pltpu.roll(ref[:, 128 * i:128 * i + 128], sh, 1) for i in (0, 1))
            return [jnp.where(m, b, a), jnp.where(m, a, b)]
        wr, wi = rolled(wr_ref), rolled(wi_ref)
        def blocks(ri, b):
            edge = po_ref[ri, 4, rows, :]
            if b == 0:
                return jnp.where(lane >= c, po_ref[ri, 0, rows, :], jnp.where(lane + 256 >= c, po_ref[ri, 2, rows, :], edge))
            return jnp.where(lane - 128 >= c, edge, jnp.where(lane + 128 >= c, po_ref[ri, 1, rows, :], po_ref[ri, 3, rows, :]))
        amp = permuted_amp(frames_ref[idx_ref[s]])
        t_re, t_im = slot_terms(blocks, wr, wi, amp, tab_ref)
        power = [wr[i] * wr[i] + wi[i] * wi[i] for i in (0, 1)]
        cols = [lane + 128 * b for b in range(4)] + [jnp.where(lane < 64, lane + 512, lane - 128)]
        masks = [(col >= c) & (col < c + 256) for col in cols]
        for out, t in ((acc_ref.at[0], t_re), (acc_ref.at[1], t_im), (light_ref, power)):
            for b in range(5):
                src = t[b % 2] if b < 4 else jnp.where(lane < 64, t[0], t[1])
                out[b, rows, :] += jnp.where(masks[b], src, 0.0)
        return 0
    lax.fori_loop(0, count_ref[0], step, 0)

def compute(count, off, idx, po, frames, wr, wi, tab):
    smem = pl.BlockSpec(memory_space=pltpu.SMEM)
    vmem = pl.BlockSpec(memory_space=pltpu.VMEM)
    return pl.pallas_call(
        kernel,
        out_shape=(jax.ShapeDtypeStruct((2, 5, 448, 128), F32), jax.ShapeDtypeStruct((5, 448, 128), F32)),
        in_specs=[smem] * 3 + [vmem] * 5,
        out_specs=(vmem, vmem),
        compiler_params=pltpu.CompilerParams(vmem_limit_bytes=60 << 20),
    )(count, off, idx, po, frames, wr, wi, tab)

def packed(wide):
    left, right = wide[..., :HALO], wide[..., -HALO:]
    edge = jnp.concatenate([right, jnp.zeros(wide.shape[:-1] + (64,), F32), left], axis=-1)
    tiles = [wide[..., HALO + 128 * b : HALO + 128 * b + 128] for b in range(4)]
    return jnp.stack(tiles + [edge], axis=1)


def shards(object_re, object_im, probe_re, probe_im, frames, counts, offsets, frame_index):
    tile_r, tile_c = object_re.shape
    stacked = jnp.stack([object_re, object_im])
    padded = padded_2(stacked, (("row", 1), ("col", 2)), HALO)
    acc, light = compute(
        counts.reshape(1), offsets.reshape(16), frame_index.reshape(8), packed(padded),
        frames[0, 0], probe_re, probe_im, jnp.asarray(tables()),
    )
    acc = jnp.concatenate([acc, light[None]], axis=0)
    edge = acc[:, 4]
    acc = jnp.concatenate([edge[..., 96:]] + [acc[:, b] for b in range(4)] + [edge[..., :HALO]], axis=-1)
    from_below = passed_along(acc[:, :HALO, :], "row", -1)
    from_above = passed_along(acc[:, HALO + tile_r :, :], "row", 1)
    acc = acc.at[:, tile_r : tile_r + HALO, :].add(from_below)
    acc = acc.at[:, HALO : 2 * HALO, :].add(from_above)
    middle = acc[:, HALO : HALO + tile_r, :]
    from_right = passed_along(middle[:, :, :HALO], "col", -1)
    from_left = passed_along(middle[:, :, HALO + tile_c :], "col", 1)
    middle = middle.at[:, :, tile_c : tile_c + HALO].add(from_right)
    middle = middle.at[:, :, HALO : 2 * HALO].add(from_left)
    inner = middle[:, :, HALO : HALO + tile_c]
    denom = inner[2] + ridge
    return (object_re - inner[0] / denom, object_im - inner[1] / denom)


def solution(mesh):
    return jax.shard_map(
        shards,
        mesh=mesh,
        in_specs=(
            P("row", "col"),
            P("row", "col"),
            P(),
            P(),
            P("row", "col", None, None, None),
            P("row", "col"),
            P("row", "col", None, None),
            P("row", "col", None),
        ),
        out_specs=(P("row", "col"), P("row", "col")),
        check_vma=False,
    )
```

```python
import jax
import jax.numpy as jnp
import numpy as np
from jax import lax
from jax.experimental import pallas as pl
from jax.experimental.pallas import tpu as pltpu
from jax.sharding import PartitionSpec as P

F32, BF16 = jnp.float32, jnp.bfloat16
HALO, TR, TC, PS, SLOTS = 32, 384, 512, 256, 8
WIDE = TR + 2 * HALO
SIDES = ((-1, 0), (1, 0), (0, -1), (0, 1), (-1, -1), (-1, 1), (1, -1), (1, 1))
BACK = tuple(SIDES.index((-r, -c)) for r, c in SIDES)


def tables():
    n = np.arange(128)[:, None]
    k = np.arange(128)[None, :]
    out = []
    for angle in (2 * np.pi * (n * k % 128) / 128, 2 * np.pi * (n * (2 * k + 1) % 256) / 256):
        c, s = np.cos(angle) / 16, np.sin(angle) / 16
        m = np.block([[c, -s], [s, c]])
        out += [m, m.T]
    full = np.stack(out)
    hi = full.astype(np.float32).astype(BF16)
    lo = (full - hi.astype(np.float64)).astype(np.float32).astype(BF16)
    return np.stack([hi, lo], axis=1)


def split(x):
    hi = x.astype(BF16)
    lo = (x - hi.astype(F32)).astype(BF16)
    return hi, lo


def dot(a, b):
    return jnp.dot(a, b, preferred_element_type=F32)


def right(x, tab, t):
    hi, lo = split(x)
    th, tl = tab[t, 0], tab[t, 1]
    return dot(jnp.concatenate([hi, lo, hi], 1), jnp.concatenate([th, th, tl], 0))


def left(x, tab, t):
    hi, lo = split(x)
    th, tl = tab[t, 0], tab[t, 1]
    return dot(jnp.concatenate([th, th, tl], 1), jnp.concatenate([hi, lo, hi], 0))


def slot_terms(blocks, wr, wi, amp, tab):
    e_re = [wr[b] * blocks[0][b] - wi[b] * blocks[1][b] for b in (0, 1)]
    e_im = [wr[b] * blocks[1][b] + wi[b] * blocks[0][b] for b in (0, 1)]
    even = right(jnp.concatenate([e_re[0] + e_re[1], e_im[0] + e_im[1]], 1), tab, 0)
    odd = right(jnp.concatenate([e_re[0] - e_re[1], e_im[0] - e_im[1]], 1), tab, 2)

    def halves(op):
        a, b = op(even[:128], even[128:]), op(odd[:128], odd[128:])
        re = jnp.concatenate([a[:, :128], b[:, :128]], 1)
        im = jnp.concatenate([a[:, 128:], b[:, 128:]], 1)
        return jnp.concatenate([re, im], 0)

    u = left(halves(lambda p, q: p + q), tab, 1)
    v = left(halves(lambda p, q: p - q), tab, 3)

    def scaled(f, a):
        re, im = f[:128], f[128:]
        factor = 1.0 - a * lax.rsqrt(jnp.maximum(re * re + im * im, 0.25))
        return jnp.concatenate([re * factor, im * factor], 0)

    a = left(scaled(u, amp[:128]), tab, 0)
    b = left(scaled(v, amp[128:]), tab, 2)
    top, bot = a + b, a - b
    re = jnp.concatenate([top[:128], bot[:128]], 0)
    im = jnp.concatenate([top[128:], bot[128:]], 0)
    a = right(jnp.concatenate([re[:, :128], im[:, :128]], 1), tab, 1)
    b = right(jnp.concatenate([re[:, 128:], im[:, 128:]], 1), tab, 3)
    back = (a + b, a - b)
    t_re = [wr[i] * back[i][:, :128] + wi[i] * back[i][:, 128:] for i in (0, 1)]
    t_im = [wr[i] * back[i][:, 128:] - wi[i] * back[i][:, :128] for i in (0, 1)]
    return t_re, t_im


def permuted_amp(frame):
    r = lax.broadcasted_iota(jnp.int32, (PS, PS), 0)
    c = lax.broadcasted_iota(jnp.int32, (PS, PS), 1)

    def order(j):
        return jnp.where(j < 128, 2 * j, 2 * j - 255)

    cols = (r == order(c)).astype(F32).astype(BF16)
    rows = (c == order(r)).astype(F32).astype(BF16)
    return jnp.sqrt(dot(rows, dot(frame, cols).astype(BF16)))


def lanes(rows):
    return lax.broadcasted_iota(jnp.int32, (rows, 128), 1)


def turned(x, by):
    return pltpu.roll(x, by % 128, 1) if by % 128 else x


def pack(x, high):
    rows = x.shape[0] // 4
    lane = lanes(rows)
    out = None
    for g in range(4):
        piece = turned(x[rows * g : rows * (g + 1)], 32 * (g + 1) if high else 32 * g)
        out = piece if out is None else jnp.where(lane >= 32 * g, piece, out)
    return out


def unpack(x, high):
    return jnp.concatenate([turned(x, 96 - 32 * g if high else -32 * g) for g in range(4)], 0)


def kernel(
    count_ref, off_ref, idx_ref, obj_re, obj_im, probe_re, probe_im, frames_hbm, tab_hbm,
    new_re, new_im,
    po, acc, light, term, amp, wave, turns, frames, tab, probe,
    side_out, side_in, corner_out, corner_in,
    lrow_in, lside_out, lside_in, lcorner_out, lcorner_in,
    grow_in, gside_out, gside_in, gcorner_out, gcorner_in,
    local_sem, send_sem, recv_sem,
):
    row, col = lax.axis_index("row"), lax.axis_index("col")
    n_row, n_col = lax.axis_size("row"), lax.axis_size("col")
    peers = [(row + dr, col + dc) for dr, dc in SIDES]
    there = []
    for dr, dc in SIDES:
        ok = []
        if dr:
            ok.append(row > 0 if dr < 0 else row < n_row - 1)
        if dc:
            ok.append(col > 0 if dc < 0 else col < n_col - 1)
        there.append(ok[0] if len(ok) == 1 else ok[0] & ok[1])

    barrier = pltpu.get_barrier_semaphore()
    for k in range(8):
        @pl.when(there[k])
        def _():
            pl.semaphore_signal(barrier, inc=1, device_id=peers[k], device_id_type=pl.DeviceIdType.MESH)

    loads = []
    for b in range(4):
        for i, source in enumerate((obj_re, obj_im)):
            loads.append((source.at[:, :, pl.ds(128 * b, 128)], po.at[i, b, 2:26]))
    loads += [(probe_re, probe.at[0]), (probe_im, probe.at[1]), (frames_hbm, frames), (tab_hbm, tab)]
    loads = [pltpu.make_async_copy(s, d, local_sem.at[i]) for i, (s, d) in enumerate(loads)]
    for load in loads:
        load.start()

    for k, (dr, dc) in enumerate(SIDES):
        @pl.when(jnp.logical_not(there[k]))
        def _():
            if dc == 0:
                at = 0 if dr < 0 else HALO + TR
                po[:, 0:4, at // 16 : at // 16 + 2] = jnp.zeros((2, 4, 2, 16, 128), F32)
                h = 0 if dr < 0 else 1
                lrow_in[h] = jnp.zeros((1, 4, HALO, 128), F32)
                grow_in[h] = jnp.zeros((2, 4, HALO, 128), F32)
            elif dr == 0:
                for ref in (side_in, lside_in, gside_in):
                    ref[k - 2] = jnp.zeros(ref.shape[1:], F32)
            else:
                for ref in (corner_in, lcorner_in, gcorner_in):
                    ref[k - 4] = jnp.zeros(ref.shape[1:], F32)

    acc[...] = jnp.zeros_like(acc)
    light[...] = jnp.zeros_like(light)
    term[:, :, 0:12] = jnp.zeros((2, 2, 12, 16, 128), F32)
    term[:, :, 28:40] = jnp.zeros((2, 2, 12, 16, 128), F32)

    def message(phase, k, source, target):
        return pltpu.make_async_remote_copy(
            src_ref=source,
            dst_ref=target,
            send_sem=send_sem.at[phase, k],
            recv_sem=recv_sem.at[phase, BACK[k]],
            device_id=peers[k],
            device_id_type=pl.DeviceIdType.MESH,
        )

    def messages(phase, rows_of, side_o, side_i, corner_o, corner_i):
        out = []
        for k, (dr, dc) in enumerate(SIDES):
            j = BACK[k]
            if dc == 0:
                out.append(message(phase, k, *rows_of(k)))
            elif dr == 0:
                out.append(message(phase, k, side_o.at[k - 2], side_i.at[j - 2]))
            else:
                out.append(message(phase, k, corner_o.at[k - 4], corner_i.at[j - 4]))
        return out

    def start(group):
        for k in range(8):
            @pl.when(there[k])
            def _():
                group[k].start()

    def arrive(group):
        for k in range(8):
            @pl.when(there[k])
            def _():
                group[BACK[k]].wait_recv()

    def drain(group):
        for k in range(8):
            @pl.when(there[k])
            def _():
                group[k].wait_send()

    def object_rows(k):
        if k == 0:
            return po.at[:, 0:4, 2:4], po.at[:, 0:4, 26:28]
        return po.at[:, 0:4, 24:26], po.at[:, 0:4, 0:2]

    def spilled_rows(ref, into):
        def rows_of(k):
            at = 0 if k == 0 else HALO + TR
            return ref.at[:, 0:4, at : at + HALO, :], into.at[1 - k]
        return rows_of

    objects = messages(0, object_rows, side_out, side_in, corner_out, corner_in)
    lights = messages(1, spilled_rows(light, lrow_in), lside_out, lside_in, lcorner_out, lcorner_in)
    grads = messages(2, spilled_rows(acc, grow_in), gside_out, gside_in, gcorner_out, gcorner_in)

    for load in loads[:8]:
        load.wait()
    for i in range(2):
        side_out[0, i] = pack(po[i, 0, 2:26].reshape(TR, 128), False)
        side_out[1, i] = pack(po[i, 3, 2:26].reshape(TR, 128), True)
        for k in range(4, 8):
            dr, dc = SIDES[k]
            at = 2 if dr < 0 else 24
            corner_out[k - 4, i] = pack(po[i, 0 if dc < 0 else 3, at : at + 2].reshape(HALO, 128), dc > 0)

    neighbours = sum(t.astype(jnp.int32) for t in there)
    pl.semaphore_wait(barrier, neighbours)
    start(objects)
    for load in loads[8:]:
        load.wait()

    for i in range(2):
        for h in range(2):
            for k in range(8):
                turns[k, i, h] = turned(probe[i, :, 128 * h : 128 * h + 128], 16 * k)
    count = count_ref[0, 0]

    def place(s):
        p = lax.div(off_ref[0, s] + HALO, 16)
        c = off_ref[1, s]
        live = lax.max(lax.min(count - s, 1), 0)
        return p, c, c + PS * live

    def add(into, i, p, c, end):
        rows = pl.ds(12 - p, 28)
        lane = lanes(WIDE)
        cols = [lane + 128 * b for b in range(4)] + [jnp.where(lane < 64, lane + 512, lane - 128)]
        got = [term[i, h, rows].reshape(WIDE, 128) for h in range(2)]
        for b, at in enumerate(cols):
            source = got[b % 2] if b < 4 else jnp.where(lane < 64, got[0], got[1])
            into[i, b] += jnp.where((at >= c) & (at < end), source, 0.0)

    def prepare(s, _):
        p, c, end = place(s)
        amp[s] = permuted_amp(frames[idx_ref[0, s]])
        lane = lanes(PS)
        turn = lax.rem(c + PS, PS)
        by = lax.rem(turn, 128)
        swap = lax.div(turn, 128)
        other = (1 - 2 * swap) * (lane - by) - swap < 0
        kept = []
        for i in range(2):
            a, b = (turns[lax.div(by, 16), i, h] for h in (0, 1))
            kept.append((jnp.where(other, b, a), jnp.where(other, a, b)))
            for h in range(2):
                wave[s, i, h] = kept[i][h]
        for h in range(2):
            power = kept[0][h] * kept[0][h] + kept[1][h] * kept[1][h]
            term[0, h, 12:28] = power.reshape(16, 16, 128)
        add(light, 0, p, c, end)
        return 0

    lax.fori_loop(0, SLOTS, prepare, 0)

    def pack_spill(ref, side_o, corner_o):
        for i in range(ref.shape[0]):
            for h in range(2):
                side_o[h, i] = pack(ref[i, 4, HALO : HALO + TR, :], h == 0)
            for k in range(4, 8):
                dr, dc = SIDES[k]
                at = 0 if dr < 0 else HALO + TR
                corner_o[k - 4, i] = pack(ref[i, 4, at : at + HALO, :], dc < 0)

    pack_spill(light, lside_out, lcorner_out)

    arrive(objects)
    for i in range(2):
        for at, rows, low, high in (
            (0, HALO, corner_in[1, i], corner_in[0, i]),
            (HALO, TR, side_in[1, i], side_in[0, i]),
            (HALO + TR, HALO, corner_in[3, i], corner_in[2, i]),
        ):
            edge = jnp.where(lanes(rows) < 64, unpack(low, False), unpack(high, True))
            po[i, 4, at // 16 : (at + rows) // 16] = edge.reshape(rows // 16, 16, 128)
    start(lights)

    def step(s, _):
        p, c, end = place(s)
        lane = lanes(PS)
        blocks = []
        for i in range(2):
            here = [po[i, b, pl.ds(p, 16)].reshape(PS, 128) for b in range(5)]
            first = jnp.where(lane >= c, here[0], jnp.where(lane + 256 >= c, here[2], here[4]))
            second = jnp.where(lane - 128 >= c, here[4], jnp.where(lane + 128 >= c, here[1], here[3]))
            blocks.append((first, second))
        wr, wi = ([wave[s, i, h] for h in range(2)] for i in range(2))
        t_re, t_im = slot_terms(blocks, wr, wi, amp[s], tab)
        for i, t in enumerate((t_re, t_im)):
            for h in range(2):
                term[i, h, 12:28] = t[h].reshape(16, 16, 128)
        for i in range(2):
            add(acc, i, p, c, end)
        return 0

    lax.fori_loop(0, SLOTS, step, 0)

    pack_spill(acc, gside_out, gcorner_out)
    start(grads)

    def absorb(ref, row_in, side_i, corner_i):
        for i in range(ref.shape[0]):
            for h, at in ((0, HALO), (1, TR)):
                ref[i, 0:4, at : at + HALO, :] += row_in[h, i]
            for h, b in ((0, 0), (1, 3)):
                keep = lanes(TR) < 32 if h == 0 else lanes(TR) >= 96
                ref[i, b, HALO : HALO + TR, :] += jnp.where(keep, unpack(side_i[h, i], h == 1), 0.0)
            for k in range(4, 8):
                dr, dc = SIDES[k]
                at = HALO if dr < 0 else TR
                keep = lanes(HALO) < 32 if dc < 0 else lanes(HALO) >= 96
                ref[i, 0 if dc < 0 else 3, at : at + HALO, :] += jnp.where(keep, unpack(corner_i[k - 4, i], dc > 0), 0.0)

    arrive(lights)
    absorb(light, lrow_in, lside_in, lcorner_in)
    for b in range(4):
        light[0, b, HALO : HALO + TR, :] = 1.0 / (light[0, b, HALO : HALO + TR, :] + 1.0)
    arrive(grads)
    absorb(acc, grow_in, gside_in, gcorner_in)
    for i, out in enumerate((new_re, new_im)):
        for b in range(4):
            rows = pl.ds(HALO, TR)
            out[:, 128 * b : 128 * b + 128] = po[i, b, 2:26].reshape(TR, 128) - acc[i, b, rows, :] * light[0, b, rows, :]
    for group in (objects, lights, grads):
        drain(group)


def shards(object_re, object_im, probe_re, probe_im, frames, counts, offsets, frame_index):
    smem = pl.BlockSpec(memory_space=pltpu.SMEM)
    anywhere = pl.BlockSpec(memory_space=pl.ANY)
    vmem = pl.BlockSpec(memory_space=pltpu.VMEM)
    spills = []
    for n in (1, 2):
        spills += [
            pltpu.VMEM((2, n, 4, HALO, 128), F32),
            pltpu.VMEM((2, n, 96, 128), F32),
            pltpu.VMEM((2, n, 96, 128), F32),
            pltpu.VMEM((4, n, 8, 128), F32),
            pltpu.VMEM((4, n, 8, 128), F32),
        ]
    return pl.pallas_call(
        kernel,
        out_shape=(jax.ShapeDtypeStruct((TR, TC), F32),) * 2,
        in_specs=[smem] * 3 + [anywhere] * 6,
        out_specs=(vmem, vmem),
        scratch_shapes=[
            pltpu.VMEM((2, 5, 28, 16, 128), F32),
            pltpu.VMEM((2, 5, WIDE, 128), F32),
            pltpu.VMEM((1, 5, WIDE, 128), F32),
            pltpu.VMEM((2, 2, 40, 16, 128), F32),
            pltpu.VMEM((SLOTS, PS, PS), F32),
            pltpu.VMEM((SLOTS, 2, 2, PS, 128), F32),
            pltpu.VMEM((8, 2, 2, PS, 128), F32),
            pltpu.VMEM((8, PS, PS), BF16),
            pltpu.VMEM((4, 2, PS, PS), BF16),
            pltpu.VMEM((2, PS, PS), F32),
            pltpu.VMEM((2, 2, 96, 128), F32),
            pltpu.VMEM((2, 2, 96, 128), F32),
            pltpu.VMEM((4, 2, 8, 128), F32),
            pltpu.VMEM((4, 2, 8, 128), F32),
            *spills,
            pltpu.SemaphoreType.DMA((12,)),
            pltpu.SemaphoreType.DMA((3, 8)),
            pltpu.SemaphoreType.DMA((3, 8)),
        ],
        compiler_params=pltpu.CompilerParams(
            collective_id=0, has_side_effects=True, vmem_limit_bytes=63 << 20
        ),
    )(
        counts, offsets[0, 0].T, frame_index.reshape(1, SLOTS),
        object_re.reshape(24, 16, TC), object_im.reshape(24, 16, TC), probe_re, probe_im, frames.reshape(8, PS, PS), jnp.asarray(tables()),
    )


def solution(mesh):
    return jax.shard_map(
        shards,
        mesh=mesh,
        in_specs=(
            P("row", "col"),
            P("row", "col"),
            P(),
            P(),
            P("row", "col", None, None, None),
            P("row", "col"),
            P("row", "col", None, None),
            P("row", "col", None),
        ),
        out_specs=(P("row", "col"), P("row", "col")),
        check_vma=False,
    )
```

```python
import jax
import jax.numpy as jnp
import numpy as np
from jax import lax
from jax.experimental import pallas as pl
from jax.experimental.pallas import tpu as pltpu
from jax.sharding import PartitionSpec as P

F32, BF16 = jnp.float32, jnp.bfloat16
HALO, TR, TC, PS, SLOTS = 32, 384, 512, 256, 8
ROWS = 32
WIDE = TR + 2 * HALO
SIDES = ((-1, 0), (1, 0), (0, -1), (0, 1), (-1, -1), (-1, 1), (1, -1), (1, 1))
BACK = tuple(SIDES.index((-r, -c)) for r, c in SIDES)


def tables():
    n = np.arange(128)[:, None]
    k = np.arange(128)[None, :]
    out = []
    for angle in (2 * np.pi * (n * k % 128) / 128, 2 * np.pi * (n * (2 * k + 1) % 256) / 256):
        c, s = np.cos(angle) / 16, np.sin(angle) / 16
        m = np.block([[c, -s], [s, c]])
        out += [m, m.T]
    full = np.stack(out)
    hi = full.astype(np.float32).astype(BF16)
    lo = (full - hi.astype(np.float64)).astype(np.float32).astype(BF16)
    return np.stack([hi, lo], axis=1)


def split(x):
    hi = x.astype(BF16)
    lo = (x - hi.astype(F32)).astype(BF16)
    return hi, lo


def dot(a, b):
    return jnp.dot(a, b, preferred_element_type=F32)


def right(x, tab, t):
    hi, lo = x
    th, tl = tab[t, 0], tab[t, 1]
    return dot(jnp.concatenate([hi, lo, hi], 1), jnp.concatenate([th, th, tl], 0))


def left(x, tab, t):
    hi, lo = x
    th, tl = tab[t, 0], tab[t, 1]
    return dot(jnp.concatenate([th, th, tl], 1), jnp.concatenate([hi, lo, hi], 0))


def slot_terms(patch, wave, amp, tab, keep):
    wr, wi = wave()
    blocks = patch()
    e_re = [wr[b] * blocks[0][b] - wi[b] * blocks[1][b] for b in (0, 1)]
    e_im = [wr[b] * blocks[1][b] + wi[b] * blocks[0][b] for b in (0, 1)]
    even = jnp.concatenate([e_re[0] + e_re[1], e_im[0] + e_im[1]], 1)
    odd = jnp.concatenate([e_re[0] - e_re[1], e_im[0] - e_im[1]], 1)
    even, odd = split(even), split(odd)
    yield
    even = right(even, tab, 0)
    odd = right(odd, tab, 2)
    yield

    def halves(op):
        a, b = op(even[:128], even[128:]), op(odd[:128], odd[128:])
        re = jnp.concatenate([a[:, :128], b[:, :128]], 1)
        im = jnp.concatenate([a[:, 128:], b[:, 128:]], 1)
        return jnp.concatenate([re, im], 0)

    u, v = split(halves(lambda p, q: p + q)), split(halves(lambda p, q: p - q))
    yield
    u = left(u, tab, 1)
    v = left(v, tab, 3)
    yield

    def scaled(f, a):
        re, im = f[:128], f[128:]
        factor = 1.0 - a * lax.rsqrt(jnp.maximum(re * re + im * im, 0.25))
        return split(jnp.concatenate([re * factor, im * factor], 0))

    a, b = amp()
    u, v = scaled(u, a), scaled(v, b)
    yield
    a = left(u, tab, 0)
    b = left(v, tab, 2)
    yield
    top, bot = a + b, a - b
    re = jnp.concatenate([top[:128], bot[:128]], 0)
    im = jnp.concatenate([top[128:], bot[128:]], 0)
    u = split(jnp.concatenate([re[:, :128], im[:, :128]], 1))
    v = split(jnp.concatenate([re[:, 128:], im[:, 128:]], 1))
    yield
    a = right(u, tab, 1)
    b = right(v, tab, 3)
    yield
    back = (a + b, a - b)
    wr, wi = wave()
    for i in (0, 1):
        keep(0, i, wr[i] * back[i][:, :128] + wi[i] * back[i][:, 128:])
        keep(1, i, wr[i] * back[i][:, 128:] - wi[i] * back[i][:, :128])
    yield


def orders():
    r = lax.broadcasted_iota(jnp.int32, (PS, PS), 0)
    c = lax.broadcasted_iota(jnp.int32, (PS, PS), 1)

    def order(j):
        return jnp.where(j < 128, 2 * j, 2 * j - 255)

    return (r == order(c)).astype(F32).astype(BF16), (c == order(r)).astype(F32).astype(BF16)


def lanes(rows):
    return lax.broadcasted_iota(jnp.int32, (rows, 128), 1)


def turned(x, by):
    return pltpu.roll(x, by % 128, 1) if by % 128 else x


def pack(x, high):
    rows = x.shape[0] // 4
    lane = lanes(rows)
    out = None
    for g in range(4):
        piece = turned(x[rows * g : rows * (g + 1)], 32 * (g + 1) if high else 32 * g)
        out = piece if out is None else jnp.where(lane >= 32 * g, piece, out)
    return out


def unpack(x, high):
    return jnp.concatenate([turned(x, 96 - 32 * g if high else -32 * g) for g in range(4)], 0)


def kernel(
    count_ref, off_ref, idx_ref, obj_re, obj_im, probe_re, probe_im, frames_hbm, tab_hbm,
    new_re, new_im,
    po, acc, light, term, amp, wave, turns, frames, tab, probe, swaps, base,
    side_out, side_in, corner_out, corner_in,
    lrow_in, lside_out, lside_in, lcorner_out, lcorner_in,
    grow_in, gside_out, gside_in, gcorner_out, gcorner_in,
    local_sem, send_sem, recv_sem,
):
    row, col = lax.axis_index("row"), lax.axis_index("col")
    n_row, n_col = lax.axis_size("row"), lax.axis_size("col")
    peers = [(row + dr, col + dc) for dr, dc in SIDES]
    there = []
    for dr, dc in SIDES:
        ok = []
        if dr:
            ok.append(row > 0 if dr < 0 else row < n_row - 1)
        if dc:
            ok.append(col > 0 if dc < 0 else col < n_col - 1)
        there.append(ok[0] if len(ok) == 1 else ok[0] & ok[1])

    barrier = pltpu.get_barrier_semaphore()
    for k in range(8):
        @pl.when(there[k])
        def _():
            pl.semaphore_signal(barrier, inc=1, device_id=peers[k], device_id_type=pl.DeviceIdType.MESH)

    loads = []
    for b in range(4):
        for i, source in enumerate((obj_re, obj_im)):
            loads.append((source.at[:, :, pl.ds(128 * b, 128)], po.at[i, b + 1, 2:26]))
    loads += [(probe_re, probe.at[0]), (probe_im, probe.at[1]), (frames_hbm, frames), (tab_hbm, tab)]
    loads = [pltpu.make_async_copy(s, d, local_sem.at[i]) for i, (s, d) in enumerate(loads)]
    for load in loads:
        load.start()

    def message(phase, k, source, target):
        return pltpu.make_async_remote_copy(
            src_ref=source,
            dst_ref=target,
            send_sem=send_sem.at[phase, k],
            recv_sem=recv_sem.at[phase, BACK[k]],
            device_id=peers[k],
            device_id_type=pl.DeviceIdType.MESH,
        )

    def messages(phase, rows_of, side_o, side_i, corner_o, corner_i):
        out = []
        for k, (dr, dc) in enumerate(SIDES):
            j = BACK[k]
            if dc == 0:
                out.append(message(phase, k, *rows_of(k)))
            elif dr == 0:
                out.append(message(phase, k, side_o.at[k - 2], side_i.at[j - 2]))
            else:
                out.append(message(phase, k, corner_o.at[k - 4], corner_i.at[j - 4]))
        return out

    def start(group):
        for k in range(8):
            @pl.when(there[k])
            def _():
                group[k].start()

    def arrive(group):
        for k in range(8):
            @pl.when(there[k])
            def _():
                group[BACK[k]].wait_recv()

    def drain(group):
        for k in range(8):
            @pl.when(there[k])
            def _():
                group[k].wait_send()

    def object_rows(k):
        if k == 0:
            return po.at[:, 1:5, 2:4], po.at[:, 1:5, 26:28]
        return po.at[:, 1:5, 24:26], po.at[:, 1:5, 0:2]

    def spilled_rows(ref, into):
        def rows_of(k):
            at = 0 if k == 0 else HALO + TR
            return ref.at[:, 0:4, at : at + HALO, :], into.at[1 - k]
        return rows_of

    objects = messages(0, object_rows, side_out, side_in, corner_out, corner_in)
    lights = messages(1, spilled_rows(light, lrow_in), lside_out, lside_in, lcorner_out, lcorner_in)
    grads = messages(2, spilled_rows(acc, grow_in), gside_out, gside_in, gcorner_out, gcorner_in)

    for load in loads[:8]:
        load.wait()
    for i in range(2):
        side_out[0, i] = pack(po[i, 1, 2:26].reshape(TR, 128), False)
        side_out[1, i] = pack(po[i, 4, 2:26].reshape(TR, 128), True)
        for k in range(4, 8):
            dr, dc = SIDES[k]
            at = 2 if dr < 0 else 24
            corner_out[k - 4, i] = pack(po[i, 1 if dc < 0 else 4, at : at + 2].reshape(HALO, 128), dc > 0)

    neighbours = sum(t.astype(jnp.int32) for t in there)
    pl.semaphore_wait(barrier, neighbours)
    start(objects)

    for k, (dr, dc) in enumerate(SIDES):
        @pl.when(jnp.logical_not(there[k]))
        def _():
            if dc == 0:
                at = 0 if dr < 0 else 26
                po[:, 1:5, at : at + 2] = jnp.zeros((2, 4, 2, 16, 128), F32)
                h = 0 if dr < 0 else 1
                lrow_in[h] = jnp.zeros((1, 4, HALO, 128), F32)
                grow_in[h] = jnp.zeros((2, 4, HALO, 128), F32)
            elif dr == 0:
                for ref in (side_in, lside_in, gside_in):
                    ref[k - 2] = jnp.zeros(ref.shape[1:], F32)
            else:
                for ref in (corner_in, lcorner_in, gcorner_in):
                    ref[k - 4] = jnp.zeros(ref.shape[1:], F32)

    def clear(j, _):
        for i in range(2):
            term[i, pl.ds(40 * j, 12)] = jnp.zeros((12, 16, 128), F32)
            term[i, pl.ds(40 * j + 28, 12)] = jnp.zeros((12, 16, 128), F32)
        return 0

    lax.fori_loop(0, 3 * SLOTS + 1, clear, 0)
    for i in range(2):
        term[i, 120 * SLOTS + 12 : 120 * SLOTS + 28] = jnp.zeros((16, 16, 128), F32)
    swaps[0], swaps[1] = orders()

    for load in loads[8:]:
        load.wait()
    for i in range(2):
        for h in range(2):
            for k in range(8):
                turns[k, i, h] = turned(probe[i, :, 128 * h : 128 * h + 128], 16 * k)
    count = count_ref[0, 0]

    def unit(x):
        return lax.max(lax.min(x, 1), 0)

    def place(s):
        p = lax.div(off_ref[0, s] + HALO, 16)
        c = off_ref[1, s] + 128
        return p, lax.div(c, 128), lax.rem(c, 128)

    for s in range(SLOTS):
        p, q, _ = place(s)
        for b in range(6):
            j = b - q
            inside = unit(j + 1) * unit(3 - j) * unit(count - s)
            block = 3 * SLOTS + inside * (3 * s + j - 3 * SLOTS)
            base[6 * s + b] = 40 * block + 12 - p

    def total(i, b, at, groups):
        out = None
        for s in range(SLOTS):
            piece = term[i, pl.ds(base[6 * s + b] + at, groups)]
            out = piece if out is None else out + piece
        return out.reshape(16 * groups, 128)

    def spill(into, i):
        for b in range(4):
            for at in (0, 26):
                into[i, b, 16 * at : 16 * at + 32, :] = total(i, b + 1, at, 2)

        def edge(g, _):
            both = jnp.where(lanes(64) < 64, total(i, 5, 4 * g, 4), total(i, 0, 4 * g, 4))
            into[i, 4, pl.ds(pl.multiple_of(64 * g, 64), 64), :] = both
            return 0

        lax.fori_loop(0, 7, edge, 0)

    def inner(into, i):
        def rows(g, _):
            for b in range(4):
                into[i, b, pl.ds(pl.multiple_of(HALO + 64 * g, 32), 64), :] = total(i, b + 1, 2 + 4 * g, 4)
            return 0

        lax.fori_loop(0, 6, rows, 0)

    def keep(s, i, r, at, h, value):
        def at_block(j):
            return pl.ds(120 * s + (40 * j + 12 + at // 16), value.shape[0] // 16)

        shape = (value.shape[0] // 16, 16, 128)
        if h == 1:
            term[i, at_block(1)] = value.reshape(shape)
            return
        mine = lanes(value.shape[0]) >= r
        term[i, at_block(0)] = jnp.where(mine, value, 0.0).reshape(shape)
        term[i, at_block(2)] = jnp.where(mine, 0.0, value).reshape(shape)

    def prepare(s, _):
        _, _, r = place(s)
        mixed = dot(frames[idx_ref[0, s]], swaps[0]).astype(BF16)
        amp[s] = jnp.sqrt(dot(swaps[1], mixed))
        by = lax.div(r, 16)
        for at in range(0, PS, ROWS):
            rows = slice(at, at + ROWS)
            other = lanes(ROWS) < r
            kept = []
            for i in range(2):
                a, b = (turns[by, i, h, rows, :] for h in (0, 1))
                kept.append((jnp.where(other, b, a), jnp.where(other, a, b)))
                for h in range(2):
                    wave[s, i, h, rows, :] = kept[i][h]
            for h in range(2):
                keep(s, 0, r, at, h, kept[0][h] * kept[0][h] + kept[1][h] * kept[1][h])
        return 0

    lax.fori_loop(0, SLOTS, prepare, 0)
    spill(light, 0)
    inner(light, 0)

    def pack_spill(ref, side_o, corner_o):
        for i in range(ref.shape[0]):
            for h in range(2):
                side_o[h, i] = pack(ref[i, 4, HALO : HALO + TR, :], h == 0)
            for k in range(4, 8):
                dr, dc = SIDES[k]
                at = 0 if dr < 0 else HALO + TR
                corner_o[k - 4, i] = pack(ref[i, 4, at : at + HALO, :], dc < 0)

    pack_spill(light, lside_out, lcorner_out)

    arrive(objects)
    for i in range(2):
        for at, rows, low, high in (
            (0, HALO, corner_in[1, i], corner_in[0, i]),
            (HALO, TR, side_in[1, i], side_in[0, i]),
            (HALO + TR, HALO, corner_in[3, i], corner_in[2, i]),
        ):
            for b, side in ((5, unpack(low, False)), (0, unpack(high, True))):
                po[i, b, at // 16 : (at + rows) // 16] = side.reshape(rows // 16, 16, 128)
    start(lights)

    def slot(s):
        p, q, r = place(s)

        def patch():
            out = []
            for i in range(2):
                first, middle, last = (po[i, q + j, pl.ds(p, 16)].reshape(PS, 128) for j in range(3))
                out.append((jnp.where(lanes(PS) >= r, first, last), middle))
            return out

        return slot_terms(
            patch,
            lambda: [[wave[s, i, h] for h in range(2)] for i in range(2)],
            lambda: (amp[s, 0:128], amp[s, 128:256]),
            tab,
            lambda i, h, value: keep(s, i, r, 0, h, value),
        )

    def step(j, _):
        first, second = slot(2 * j), slot(2 * j + 1)
        next(first)
        for _ in range(8):
            next(second)
            next(first)
        next(second)
        return 0

    lax.fori_loop(0, SLOTS // 2, step, 0)
    for i in range(2):
        spill(acc, i)
    pack_spill(acc, gside_out, gcorner_out)
    start(grads)
    for i in range(2):
        inner(acc, i)

    def absorb(ref, row_in, side_i, corner_i):
        for i in range(ref.shape[0]):
            for h, at in ((0, HALO), (1, TR)):
                ref[i, 0:4, at : at + HALO, :] += row_in[h, i]
            for h, b in ((0, 0), (1, 3)):
                keep = lanes(TR) < 32 if h == 0 else lanes(TR) >= 96
                ref[i, b, HALO : HALO + TR, :] += jnp.where(keep, unpack(side_i[h, i], h == 1), 0.0)
            for k in range(4, 8):
                dr, dc = SIDES[k]
                at = HALO if dr < 0 else TR
                keep = lanes(HALO) < 32 if dc < 0 else lanes(HALO) >= 96
                ref[i, 0 if dc < 0 else 3, at : at + HALO, :] += jnp.where(keep, unpack(corner_i[k - 4, i], dc > 0), 0.0)

    arrive(lights)
    absorb(light, lrow_in, lside_in, lcorner_in)
    for b in range(4):
        light[0, b, HALO : HALO + TR, :] = 1.0 / (light[0, b, HALO : HALO + TR, :] + 1.0)
    arrive(grads)
    absorb(acc, grow_in, gside_in, gcorner_in)
    for i, out in enumerate((new_re, new_im)):
        for b in range(4):
            rows = pl.ds(HALO, TR)
            out[:, 128 * b : 128 * b + 128] = po[i, b + 1, 2:26].reshape(TR, 128) - acc[i, b, rows, :] * light[0, b, rows, :]
    for group in (objects, lights, grads):
        drain(group)


def write_out(re, im, new_re, new_im, held, sem):
    into, out = [], []
    for i, (source, target) in enumerate(((re, new_re), (im, new_im))):
        for j in range(4):
            rows = pl.ds(96 * j, 96)
            into.append(pltpu.make_async_copy(source.at[rows], held.at[i, rows], sem.at[0, i, j]))
            out.append(pltpu.make_async_copy(held.at[i, rows], target.at[rows], sem.at[1, i, j]))
    for copy in into:
        copy.start()
    for before, after in zip(into, out):
        before.wait()
        after.start()
    for copy in out:
        copy.wait()


def shards(object_re, object_im, probe_re, probe_im, frames, counts, offsets, frame_index):
    smem = pl.BlockSpec(memory_space=pltpu.SMEM)
    anywhere = pl.BlockSpec(memory_space=pl.ANY)
    vmem = pl.BlockSpec(memory_space=pltpu.VMEM)
    spills = []
    for n in (1, 2):
        spills += [
            pltpu.VMEM((2, n, 4, HALO, 128), F32),
            pltpu.VMEM((2, n, 96, 128), F32),
            pltpu.VMEM((2, n, 96, 128), F32),
            pltpu.VMEM((4, n, 8, 128), F32),
            pltpu.VMEM((4, n, 8, 128), F32),
        ]
    results = pl.pallas_call(
        kernel,
        out_shape=(jax.ShapeDtypeStruct((TR, TC), F32),) * 2,
        in_specs=[smem] * 3 + [anywhere] * 6,
        out_specs=(vmem, vmem),
        scratch_shapes=[
            pltpu.VMEM((2, 6, 28, 16, 128), F32),
            pltpu.VMEM((2, 5, WIDE, 128), F32),
            pltpu.VMEM((1, 5, WIDE, 128), F32),
            pltpu.VMEM((2, 40 * (3 * SLOTS + 1), 16, 128), F32),
            pltpu.VMEM((SLOTS, PS, PS), F32),
            pltpu.VMEM((SLOTS, 2, 2, PS, 128), F32),
            pltpu.VMEM((8, 2, 2, PS, 128), F32),
            pltpu.VMEM((8, PS, PS), BF16),
            pltpu.VMEM((4, 2, PS, PS), BF16),
            pltpu.VMEM((2, PS, PS), F32),
            pltpu.VMEM((2, PS, PS), BF16),
            pltpu.SMEM((6 * SLOTS,), jnp.int32),
            pltpu.VMEM((2, 2, 96, 128), F32),
            pltpu.VMEM((2, 2, 96, 128), F32),
            pltpu.VMEM((4, 2, 8, 128), F32),
            pltpu.VMEM((4, 2, 8, 128), F32),
            *spills,
            pltpu.SemaphoreType.DMA((12,)),
            pltpu.SemaphoreType.DMA((3, 8)),
            pltpu.SemaphoreType.DMA((3, 8)),
        ],
        compiler_params=pltpu.CompilerParams(
            collective_id=0, has_side_effects=True, vmem_limit_bytes=63 << 20
        ),
    )(
        counts, offsets[0, 0].T, frame_index.reshape(1, SLOTS),
        object_re.reshape(24, 16, TC), object_im.reshape(24, 16, TC), probe_re, probe_im, frames.reshape(8, PS, PS), jnp.asarray(tables()),
    )
    return pl.pallas_call(
        write_out,
        out_shape=(jax.ShapeDtypeStruct((TR, TC), F32),) * 2,
        in_specs=[anywhere] * 2,
        out_specs=(anywhere,) * 2,
        scratch_shapes=[pltpu.VMEM((2, TR, TC), F32), pltpu.SemaphoreType.DMA((2, 2, 4))],
        compiler_params=pltpu.CompilerParams(vmem_limit_bytes=63 << 20),
    )(*results)


def solution(mesh):
    return jax.shard_map(
        shards,
        mesh=mesh,
        in_specs=(
            P("row", "col"),
            P("row", "col"),
            P(),
            P(),
            P("row", "col", None, None, None),
            P("row", "col"),
            P("row", "col", None, None),
            P("row", "col", None),
        ),
        out_specs=(P("row", "col"), P("row", "col")),
        check_vma=False,
    )
```

```python
import jax
import jax.numpy as jnp
import numpy as np
from jax import lax
from jax.experimental import pallas as pl
from jax.experimental.pallas import tpu as pltpu
from jax.sharding import PartitionSpec as P

F32, BF16 = jnp.float32, jnp.bfloat16
HALO, TR, TC, PS, SLOTS = 32, 384, 512, 256, 8
ROWS = 32
WIDE = TR + 2 * HALO
SIDES = ((-1, 0), (1, 0), (0, -1), (0, 1), (-1, -1), (-1, 1), (1, -1), (1, 1))
BACK = tuple(SIDES.index((-r, -c)) for r, c in SIDES)


def tables():
    n = np.arange(128)[:, None]
    k = np.arange(128)[None, :]
    out = []
    for angle in (2 * np.pi * (n * k % 128) / 128, 2 * np.pi * (n * (2 * k + 1) % 256) / 256):
        c, s = np.cos(angle) / 16, np.sin(angle) / 16
        m = np.block([[c, -s], [s, c]])
        out += [m, m.T]
    full = np.stack(out)
    hi = full.astype(np.float32).astype(BF16)
    lo = (full - hi.astype(np.float64)).astype(np.float32).astype(BF16)
    return np.stack([hi, lo], axis=1)


def split(x):
    hi = x.astype(BF16)
    lo = (x - hi.astype(F32)).astype(BF16)
    return hi, lo


def dot(a, b):
    return jnp.dot(a, b, preferred_element_type=F32)


def right(x, tab, t):
    hi, lo = x
    th, tl = tab[t, 0], tab[t, 1]
    return dot(jnp.concatenate([hi, lo, hi], 1), jnp.concatenate([th, th, tl], 0))


def left(x, tab, t):
    hi, lo = x
    th, tl = tab[t, 0], tab[t, 1]
    return dot(jnp.concatenate([th, th, tl], 1), jnp.concatenate([hi, lo, hi], 0))


def slot_terms(patch, wave, amp, tab, keep):
    wr, wi = wave()
    blocks = patch()
    e_re = [wr[b] * blocks[0][b] - wi[b] * blocks[1][b] for b in (0, 1)]
    e_im = [wr[b] * blocks[1][b] + wi[b] * blocks[0][b] for b in (0, 1)]
    even = jnp.concatenate([e_re[0] + e_re[1], e_im[0] + e_im[1]], 1)
    odd = jnp.concatenate([e_re[0] - e_re[1], e_im[0] - e_im[1]], 1)
    even, odd = split(even), split(odd)
    yield
    even = right(even, tab, 0)
    odd = right(odd, tab, 2)
    yield

    def halves(op):
        a, b = op(even[:128], even[128:]), op(odd[:128], odd[128:])
        re = jnp.concatenate([a[:, :128], b[:, :128]], 1)
        im = jnp.concatenate([a[:, 128:], b[:, 128:]], 1)
        return jnp.concatenate([re, im], 0)

    u, v = split(halves(lambda p, q: p + q)), split(halves(lambda p, q: p - q))
    yield
    u = left(u, tab, 1)
    v = left(v, tab, 3)
    yield

    def scaled(f, a):
        re, im = f[:128], f[128:]
        factor = 1.0 - a * lax.rsqrt(jnp.maximum(re * re + im * im, 0.25))
        return split(jnp.concatenate([re * factor, im * factor], 0))

    a, b = amp()
    u, v = scaled(u, a), scaled(v, b)
    yield
    a = left(u, tab, 0)
    b = left(v, tab, 2)
    yield
    top, bot = a + b, a - b
    re = jnp.concatenate([top[:128], bot[:128]], 0)
    im = jnp.concatenate([top[128:], bot[128:]], 0)
    u = split(jnp.concatenate([re[:, :128], im[:, :128]], 1))
    v = split(jnp.concatenate([re[:, 128:], im[:, 128:]], 1))
    yield
    a = right(u, tab, 1)
    b = right(v, tab, 3)
    yield
    back = (a + b, a - b)
    wr, wi = wave()
    for i in (0, 1):
        keep(0, i, wr[i] * back[i][:, :128] + wi[i] * back[i][:, 128:])
        keep(1, i, wr[i] * back[i][:, 128:] - wi[i] * back[i][:, :128])
    yield


def orders():
    r = lax.broadcasted_iota(jnp.int32, (PS, PS), 0)
    c = lax.broadcasted_iota(jnp.int32, (PS, PS), 1)

    def order(j):
        return jnp.where(j < 128, 2 * j, 2 * j - 255)

    return (r == order(c)).astype(F32).astype(BF16), (c == order(r)).astype(F32).astype(BF16)


def lanes(rows):
    return lax.broadcasted_iota(jnp.int32, (rows, 128), 1)


def turned(x, by):
    return pltpu.roll(x, by % 128, 1) if by % 128 else x


def pack(x, high):
    rows = x.shape[0] // 4
    lane = lanes(rows)
    out = None
    for g in range(4):
        piece = turned(x[rows * g : rows * (g + 1)], 32 * (g + 1) if high else 32 * g)
        out = piece if out is None else jnp.where(lane >= 32 * g, piece, out)
    return out


def unpack(x, high):
    return jnp.concatenate([turned(x, 96 - 32 * g if high else -32 * g) for g in range(4)], 0)


def kernel(
    count_hbm, off_hbm, idx_hbm, obj_re, obj_im, probe_re, probe_im, frames_hbm, tab_hbm,
    new_re, new_im,
    po, acc, light, term, amp, wave, turns, frames, tab, probe, swaps, base,
    side_out, side_in, corner_out, corner_in,
    lrow_in, lside_out, lside_in, lcorner_out, lcorner_in,
    grow_in, gside_out, gside_in, gcorner_out, gcorner_in,
    count_ref, off_ref, idx_ref, newv, local_sem, send_sem, recv_sem, out_sem,
):
    row, col = lax.axis_index("row"), lax.axis_index("col")
    n_row, n_col = lax.axis_size("row"), lax.axis_size("col")
    peers = [(row + dr, col + dc) for dr, dc in SIDES]
    there = []
    for dr, dc in SIDES:
        ok = []
        if dr:
            ok.append(row > 0 if dr < 0 else row < n_row - 1)
        if dc:
            ok.append(col > 0 if dc < 0 else col < n_col - 1)
        there.append(ok[0] if len(ok) == 1 else ok[0] & ok[1])

    barrier = pltpu.get_barrier_semaphore()
    for k in range(8):
        @pl.when(there[k])
        def _():
            pl.semaphore_signal(barrier, inc=1, device_id=peers[k], device_id_type=pl.DeviceIdType.MESH)

    loads = []
    for b in (0, 3, 1, 2):
        for i, source in enumerate((obj_re, obj_im)):
            loads.append((source.at[:, :, pl.ds(128 * b, 128)], po.at[i, b + 1, 2:26]))
    loads += [(probe_re, probe.at[0]), (probe_im, probe.at[1]), (frames_hbm, frames), (tab_hbm, tab)]
    loads += [(count_hbm, count_ref), (off_hbm, off_ref), (idx_hbm, idx_ref)]
    loads = [pltpu.make_async_copy(s, d, local_sem.at[i]) for i, (s, d) in enumerate(loads)]
    for load in loads:
        load.start()

    def message(phase, k, source, target):
        return pltpu.make_async_remote_copy(
            src_ref=source,
            dst_ref=target,
            send_sem=send_sem.at[phase, k],
            recv_sem=recv_sem.at[phase, BACK[k]],
            device_id=peers[k],
            device_id_type=pl.DeviceIdType.MESH,
        )

    def messages(phase, rows_of, side_o, side_i, corner_o, corner_i):
        out = []
        for k, (dr, dc) in enumerate(SIDES):
            j = BACK[k]
            if dc == 0:
                out.append(message(phase, k, *rows_of(k)))
            elif dr == 0:
                out.append(message(phase, k, side_o.at[k - 2], side_i.at[j - 2]))
            else:
                out.append(message(phase, k, corner_o.at[k - 4], corner_i.at[j - 4]))
        return out

    def start(group, some=range(8)):
        for k in some:
            @pl.when(there[k])
            def _():
                group[k].start()

    def arrive(group):
        for k in range(8):
            @pl.when(there[k])
            def _():
                group[BACK[k]].wait_recv()

    def drain(group):
        for k in range(8):
            @pl.when(there[k])
            def _():
                group[k].wait_send()

    def object_rows(k):
        if k == 0:
            return po.at[:, 1:5, 2:4], po.at[:, 1:5, 26:28]
        return po.at[:, 1:5, 24:26], po.at[:, 1:5, 0:2]

    def spilled_rows(ref, into):
        def rows_of(k):
            at = 0 if k == 0 else HALO + TR
            return ref.at[:, 0:4, at : at + HALO, :], into.at[1 - k]
        return rows_of

    objects = messages(0, object_rows, side_out, side_in, corner_out, corner_in)
    lights = messages(1, spilled_rows(light, lrow_in), lside_out, lside_in, lcorner_out, lcorner_in)
    grads = messages(2, spilled_rows(acc, grow_in), gside_out, gside_in, gcorner_out, gcorner_in)

    for load in loads[:4]:
        load.wait()
    for i in range(2):
        side_out[0, i] = pack(po[i, 1, 2:26].reshape(TR, 128), False)
        side_out[1, i] = pack(po[i, 4, 2:26].reshape(TR, 128), True)
        for k in range(4, 8):
            dr, dc = SIDES[k]
            at = 2 if dr < 0 else 24
            corner_out[k - 4, i] = pack(po[i, 1 if dc < 0 else 4, at : at + 2].reshape(HALO, 128), dc > 0)

    for load in loads[4:8]:
        load.wait()
    neighbours = sum(t.astype(jnp.int32) for t in there)
    pl.semaphore_wait(barrier, neighbours)
    start(objects)

    for k, (dr, dc) in enumerate(SIDES):
        @pl.when(jnp.logical_not(there[k]))
        def _():
            if dc == 0:
                at = 0 if dr < 0 else 26
                po[:, 1:5, at : at + 2] = jnp.zeros((2, 4, 2, 16, 128), F32)
                h = 0 if dr < 0 else 1
                lrow_in[h] = jnp.zeros((1, 4, HALO, 128), F32)
                grow_in[h] = jnp.zeros((2, 4, HALO, 128), F32)
            elif dr == 0:
                for ref in (side_in, lside_in, gside_in):
                    ref[k - 2] = jnp.zeros(ref.shape[1:], F32)
            else:
                for ref in (corner_in, lcorner_in, gcorner_in):
                    ref[k - 4] = jnp.zeros(ref.shape[1:], F32)

    def clear(j, _):
        for i in range(2):
            term[i, pl.ds(40 * j, 12)] = jnp.zeros((12, 16, 128), F32)
            term[i, pl.ds(40 * j + 28, 12)] = jnp.zeros((12, 16, 128), F32)
        return 0

    lax.fori_loop(0, 3 * SLOTS + 1, clear, 0)
    for i in range(2):
        term[i, 120 * SLOTS + 12 : 120 * SLOTS + 28] = jnp.zeros((16, 16, 128), F32)
    swaps[0], swaps[1] = orders()

    for load in loads[8:]:
        load.wait()
    for i in range(2):
        for h in range(2):
            for k in range(8):
                turns[k, i, h] = turned(probe[i, :, 128 * h : 128 * h + 128], 16 * k)
    count = count_ref[0, 0]

    def unit(x):
        return lax.max(lax.min(x, 1), 0)

    def place(s):
        p = lax.div(off_ref[0, s] + HALO, 16)
        c = off_ref[1, s] + 128
        return p, lax.div(c, 128), lax.rem(c, 128)

    for s in range(SLOTS):
        p, q, _ = place(s)
        for b in range(6):
            j = b - q
            inside = unit(j + 1) * unit(3 - j) * unit(count - s)
            block = 3 * SLOTS + inside * (3 * s + j - 3 * SLOTS)
            base[6 * s + b] = 40 * block + 12 - p

    def total(i, b, at, groups):
        out = None
        for s in range(SLOTS):
            piece = term[i, pl.ds(base[6 * s + b] + at, groups)]
            out = piece if out is None else out + piece
        return out.reshape(16 * groups, 128)

    def spill_rows(into, i):
        for b in range(4):
            for at in (0, 26):
                into[i, b, 16 * at : 16 * at + 32, :] = total(i, b + 1, at, 2)

    def spill_edge(into, i):
        def edge(g, _):
            both = jnp.where(lanes(64) < 64, total(i, 5, 4 * g, 4), total(i, 0, 4 * g, 4))
            into[i, 4, pl.ds(pl.multiple_of(64 * g, 64), 64), :] = both
            return 0

        lax.fori_loop(0, 7, edge, 0)

    def inner(into, i):
        def rows(g, _):
            for b in range(4):
                into[i, b, pl.ds(pl.multiple_of(HALO + 64 * g, 32), 64), :] = total(i, b + 1, 2 + 4 * g, 4)
            return 0

        lax.fori_loop(0, 6, rows, 0)

    def keep(s, i, r, at, h, value):
        def at_block(j):
            return pl.ds(120 * s + (40 * j + 12 + at // 16), value.shape[0] // 16)

        shape = (value.shape[0] // 16, 16, 128)
        if h == 1:
            term[i, at_block(1)] = value.reshape(shape)
            return
        mine = lanes(value.shape[0]) >= r
        term[i, at_block(0)] = jnp.where(mine, value, 0.0).reshape(shape)
        term[i, at_block(2)] = jnp.where(mine, 0.0, value).reshape(shape)

    def prepare(s, _):
        _, _, r = place(s)
        mixed = dot(frames[idx_ref[0, s]], swaps[0]).astype(BF16)
        amp[s] = jnp.sqrt(dot(swaps[1], mixed))
        by = lax.div(r, 16)
        for at in range(0, PS, ROWS):
            rows = slice(at, at + ROWS)
            other = lanes(ROWS) < r
            kept = []
            for i in range(2):
                a, b = (turns[by, i, h, rows, :] for h in (0, 1))
                kept.append((jnp.where(other, b, a), jnp.where(other, a, b)))
                for h in range(2):
                    wave[s, i, h, rows, :] = kept[i][h]
            for h in range(2):
                keep(s, 0, r, at, h, kept[0][h] * kept[0][h] + kept[1][h] * kept[1][h])
        return 0

    lax.fori_loop(0, SLOTS, prepare, 0)
    spill_rows(light, 0)
    spill_edge(light, 0)
    inner(light, 0)

    def pack_spill(ref, side_o, corner_o):
        for i in range(ref.shape[0]):
            for h in range(2):
                side_o[h, i] = pack(ref[i, 4, HALO : HALO + TR, :], h == 0)
            for k in range(4, 8):
                dr, dc = SIDES[k]
                at = 0 if dr < 0 else HALO + TR
                corner_o[k - 4, i] = pack(ref[i, 4, at : at + HALO, :], dc < 0)

    pack_spill(light, lside_out, lcorner_out)

    arrive(objects)
    for i in range(2):
        for at, rows, low, high in (
            (0, HALO, corner_in[1, i], corner_in[0, i]),
            (HALO, TR, side_in[1, i], side_in[0, i]),
            (HALO + TR, HALO, corner_in[3, i], corner_in[2, i]),
        ):
            for b, side in ((5, unpack(low, False)), (0, unpack(high, True))):
                po[i, b, at // 16 : (at + rows) // 16] = side.reshape(rows // 16, 16, 128)
    start(lights)

    def slot(s):
        p, q, r = place(s)

        def patch():
            out = []
            for i in range(2):
                first, middle, last = (po[i, q + j, pl.ds(p, 16)].reshape(PS, 128) for j in range(3))
                out.append((jnp.where(lanes(PS) >= r, first, last), middle))
            return out

        return slot_terms(
            patch,
            lambda: [[wave[s, i, h] for h in range(2)] for i in range(2)],
            lambda: (amp[s, 0:128], amp[s, 128:256]),
            tab,
            lambda i, h, value: keep(s, i, r, 0, h, value),
        )

    def step(j, _):
        first, second = slot(2 * j), slot(2 * j + 1)
        next(first)
        for _ in range(8):
            next(second)
            next(first)
        next(second)
        return 0

    lax.fori_loop(0, SLOTS // 2, step, 0)
    for i in range(2):
        spill_rows(acc, i)
    start(grads, (0, 1))
    for i in range(2):
        spill_edge(acc, i)
    pack_spill(acc, gside_out, gcorner_out)
    start(grads, range(2, 8))
    for i in range(2):
        inner(acc, i)

    def absorb(ref, row_in, side_i, corner_i):
        for i in range(ref.shape[0]):
            for h, at in ((0, HALO), (1, TR)):
                ref[i, 0:4, at : at + HALO, :] += row_in[h, i]
            for h, b in ((0, 0), (1, 3)):
                keep = lanes(TR) < 32 if h == 0 else lanes(TR) >= 96
                ref[i, b, HALO : HALO + TR, :] += jnp.where(keep, unpack(side_i[h, i], h == 1), 0.0)
            for k in range(4, 8):
                dr, dc = SIDES[k]
                at = HALO if dr < 0 else TR
                keep = lanes(HALO) < 32 if dc < 0 else lanes(HALO) >= 96
                ref[i, 0 if dc < 0 else 3, at : at + HALO, :] += jnp.where(keep, unpack(corner_i[k - 4, i], dc > 0), 0.0)

    arrive(lights)
    absorb(light, lrow_in, lside_in, lcorner_in)
    for b in range(4):
        light[0, b, HALO : HALO + TR, :] = 1.0 / (light[0, b, HALO : HALO + TR, :] + 1.0)
    rows = pl.ds(HALO, TR)
    outs = (new_re, new_im)
    for i in range(2):
        for b in range(4):
            mine = po[i, b + 1, 2:26].reshape(TR, 128) - acc[i, b, rows, :] * light[0, b, rows, :]
            newv[i, :, 128 * b : 128 * b + 128] = mine

    def leave(i, j, down, across):
        return pltpu.make_async_copy(newv.at[i, down, across], outs[i].at[down, across], out_sem.at[i, j])

    middle = pl.ds(HALO, TR - 2 * HALO)
    first = [leave(i, 0, middle, pl.ds(128, 256)) for i in range(2)]
    last = []
    for i in range(2):
        last += [leave(i, 1, pl.ds(0, HALO), pl.ds(0, TC)), leave(i, 2, pl.ds(TR - HALO, HALO), pl.ds(0, TC))]
        last += [leave(i, 3, middle, pl.ds(0, 128)), leave(i, 4, middle, pl.ds(384, 128))]
    for copy in first:
        copy.start()
    arrive(grads)
    for i in range(2):
        for h, at in ((0, 0), (1, TR - HALO)):
            for b in range(4):
                newv[i, at : at + HALO, 128 * b : 128 * b + 128] -= grow_in[h, i, b] * light[0, b, HALO + at : 2 * HALO + at, :]
        for h, b in ((0, 0), (1, 3)):
            across = slice(128 * b, 128 * b + 128)
            part = unpack(gside_in[h, i], h == 1)
            ends = [unpack(gcorner_in[2 * v + h, i], h == 1) for v in range(2)]
            low = jnp.concatenate([part[:HALO] + ends[0], part[HALO : TR - HALO], part[TR - HALO :] + ends[1]], 0)
            keep_lanes = lanes(TR) < 32 if h == 0 else lanes(TR) >= 96
            newv[i, :, across] -= jnp.where(keep_lanes, low * light[0, b, rows, :], 0.0)
    for copy in last:
        copy.start()
    for copy in first + last:
        copy.wait()
    for group in (objects, lights, grads):
        drain(group)


def write_out(re, im, new_re, new_im, held, sem):
    into, out = [], []
    for i, (source, target) in enumerate(((re, new_re), (im, new_im))):
        for j in range(8):
            rows = pl.ds(48 * j, 48)
            into.append(pltpu.make_async_copy(source.at[rows], held.at[i, rows], sem.at[0, i, j]))
            out.append(pltpu.make_async_copy(held.at[i, rows], target.at[rows], sem.at[1, i, j]))
    for copy in into:
        copy.start()
    for before, after in zip(into, out):
        before.wait()
        after.start()
    for copy in out:
        copy.wait()


def shards(object_re, object_im, probe_re, probe_im, frames, counts, offsets, frame_index):
    anywhere = pl.BlockSpec(memory_space=pl.ANY)
    spills = []
    for n in (1, 2):
        spills += [
            pltpu.VMEM((2, n, 4, HALO, 128), F32),
            pltpu.VMEM((2, n, 96, 128), F32),
            pltpu.VMEM((2, n, 96, 128), F32),
            pltpu.VMEM((4, n, 8, 128), F32),
            pltpu.VMEM((4, n, 8, 128), F32),
        ]
    results = pl.pallas_call(
        kernel,
        out_shape=(jax.ShapeDtypeStruct((TR, TC), F32),) * 2,
        in_specs=[anywhere] * 9,
        out_specs=(anywhere, anywhere),
        scratch_shapes=[
            pltpu.VMEM((2, 6, 28, 16, 128), F32),
            pltpu.VMEM((2, 5, WIDE, 128), F32),
            pltpu.VMEM((1, 5, WIDE, 128), F32),
            pltpu.VMEM((2, 40 * (3 * SLOTS + 1), 16, 128), F32),
            pltpu.VMEM((SLOTS, PS, PS), F32),
            pltpu.VMEM((SLOTS, 2, 2, PS, 128), F32),
            pltpu.VMEM((8, 2, 2, PS, 128), F32),
            pltpu.VMEM((8, PS, PS), BF16),
            pltpu.VMEM((4, 2, PS, PS), BF16),
            pltpu.VMEM((2, PS, PS), F32),
            pltpu.VMEM((2, PS, PS), BF16),
            pltpu.SMEM((6 * SLOTS,), jnp.int32),
            pltpu.VMEM((2, 2, 96, 128), F32),
            pltpu.VMEM((2, 2, 96, 128), F32),
            pltpu.VMEM((4, 2, 8, 128), F32),
            pltpu.VMEM((4, 2, 8, 128), F32),
            *spills,
            pltpu.SMEM((1, 1), jnp.int32),
            pltpu.SMEM((2, SLOTS), jnp.int32),
            pltpu.SMEM((1, SLOTS), jnp.int32),
            pltpu.VMEM((2, TR, TC), F32),
            pltpu.SemaphoreType.DMA((15,)),
            pltpu.SemaphoreType.DMA((3, 8)),
            pltpu.SemaphoreType.DMA((3, 8)),
            pltpu.SemaphoreType.DMA((2, 5)),
        ],
        compiler_params=pltpu.CompilerParams(
            collective_id=0, has_side_effects=True, vmem_limit_bytes=63 << 20
        ),
    )(
        counts, offsets[0, 0].T, frame_index.reshape(1, SLOTS),
        object_re.reshape(24, 16, TC), object_im.reshape(24, 16, TC), probe_re, probe_im, frames.reshape(8, PS, PS), jnp.asarray(tables()),
    )
    return pl.pallas_call(
        write_out,
        out_shape=(jax.ShapeDtypeStruct((TR, TC), F32),) * 2,
        in_specs=[anywhere] * 2,
        out_specs=(anywhere,) * 2,
        scratch_shapes=[pltpu.VMEM((2, TR, TC), F32), pltpu.SemaphoreType.DMA((2, 2, 8))],
        compiler_params=pltpu.CompilerParams(vmem_limit_bytes=63 << 20),
    )(*results)


def solution(mesh):
    return jax.shard_map(
        shards,
        mesh=mesh,
        in_specs=(
            P("row", "col"),
            P("row", "col"),
            P(),
            P(),
            P("row", "col", None, None, None),
            P("row", "col"),
            P("row", "col", None, None),
            P("row", "col", None),
        ),
        out_specs=(P("row", "col"), P("row", "col")),
        check_vma=False,
    )
```

```python
import jax
import jax.numpy as jnp
import numpy as np
from jax import lax
from jax.experimental import pallas as pl
from jax.experimental.pallas import tpu as pltpu
from jax.sharding import PartitionSpec as P

F32, BF16 = jnp.float32, jnp.bfloat16
HALO, TR, TC, PS, SLOTS = 32, 384, 512, 256, 8
ROWS = 32
WIDE = TR + 2 * HALO
SIDES = ((-1, 0), (1, 0), (0, -1), (0, 1), (-1, -1), (-1, 1), (1, -1), (1, 1))
BACK = tuple(SIDES.index((-r, -c)) for r, c in SIDES)


def tables():
    n = np.arange(128)[:, None]
    k = np.arange(128)[None, :]
    out = []
    for angle in (2 * np.pi * (n * k % 128) / 128, 2 * np.pi * (n * (2 * k + 1) % 256) / 256):
        c, s = np.cos(angle) / 16, np.sin(angle) / 16
        m = np.block([[c, -s], [s, c]])
        out += [m, m.T]
    full = np.stack(out)
    hi = full.astype(np.float32).astype(BF16)
    lo = (full - hi.astype(np.float64)).astype(np.float32).astype(BF16)
    return np.stack([hi, lo], axis=1)


def split(x):
    hi = x.astype(BF16)
    lo = (x - hi.astype(F32)).astype(BF16)
    return hi, lo


def dot(a, b):
    return jnp.dot(a, b, preferred_element_type=F32)


def right(x, tab, t):
    hi, lo = x
    th, tl = tab[t, 0], tab[t, 1]
    return dot(jnp.concatenate([hi, lo, hi], 1), jnp.concatenate([th, th, tl], 0))


def left(x, tab, t):
    hi, lo = x
    th, tl = tab[t, 0], tab[t, 1]
    return dot(jnp.concatenate([th, th, tl], 1), jnp.concatenate([hi, lo, hi], 0))


def slot_terms(patch, wave, amp, tab, keep):
    wr, wi = wave()
    blocks = patch()
    e_re = [wr[b] * blocks[0][b] - wi[b] * blocks[1][b] for b in (0, 1)]
    e_im = [wr[b] * blocks[1][b] + wi[b] * blocks[0][b] for b in (0, 1)]
    even = jnp.concatenate([e_re[0] + e_re[1], e_im[0] + e_im[1]], 1)
    odd = jnp.concatenate([e_re[0] - e_re[1], e_im[0] - e_im[1]], 1)
    even, odd = split(even), split(odd)
    yield
    even = right(even, tab, 0)
    odd = right(odd, tab, 2)
    yield

    def halves(op):
        a, b = op(even[:128], even[128:]), op(odd[:128], odd[128:])
        re = jnp.concatenate([a[:, :128], b[:, :128]], 1)
        im = jnp.concatenate([a[:, 128:], b[:, 128:]], 1)
        return jnp.concatenate([re, im], 0)

    u, v = split(halves(lambda p, q: p + q)), split(halves(lambda p, q: p - q))
    yield
    u = left(u, tab, 1)
    v = left(v, tab, 3)
    yield

    def scaled(f, a):
        re, im = f[:128], f[128:]
        factor = 1.0 - a * lax.rsqrt(jnp.maximum(re * re + im * im, 0.25))
        return split(jnp.concatenate([re * factor, im * factor], 0))

    a, b = amp()
    u, v = scaled(u, a), scaled(v, b)
    yield
    a = left(u, tab, 0)
    b = left(v, tab, 2)
    yield
    top, bot = a + b, a - b
    re = jnp.concatenate([top[:128], bot[:128]], 0)
    im = jnp.concatenate([top[128:], bot[128:]], 0)
    u = split(jnp.concatenate([re[:, :128], im[:, :128]], 1))
    v = split(jnp.concatenate([re[:, 128:], im[:, 128:]], 1))
    yield
    a = right(u, tab, 1)
    b = right(v, tab, 3)
    yield
    back = (a + b, a - b)
    wr, wi = wave()
    for i in (0, 1):
        keep(0, i, wr[i] * back[i][:, :128] + wi[i] * back[i][:, 128:])
        keep(1, i, wr[i] * back[i][:, 128:] - wi[i] * back[i][:, :128])
    yield


def orders():
    r = lax.broadcasted_iota(jnp.int32, (PS, PS), 0)
    c = lax.broadcasted_iota(jnp.int32, (PS, PS), 1)

    def order(j):
        return jnp.where(j < 128, 2 * j, 2 * j - 255)

    return (r == order(c)).astype(F32).astype(BF16), (c == order(r)).astype(F32).astype(BF16)


def lanes(rows):
    return lax.broadcasted_iota(jnp.int32, (rows, 128), 1)


def turned(x, by):
    return pltpu.roll(x, by % 128, 1) if by % 128 else x


def pack(x, high):
    rows = x.shape[0] // 4
    lane = lanes(rows)
    out = None
    for g in range(4):
        piece = turned(x[rows * g : rows * (g + 1)], 32 * (g + 1) if high else 32 * g)
        out = piece if out is None else jnp.where(lane >= 32 * g, piece, out)
    return out


def unpack(x, high):
    return jnp.concatenate([turned(x, 96 - 32 * g if high else -32 * g) for g in range(4)], 0)


def kernel(
    count_hbm, off_hbm, idx_hbm, obj_re, obj_im, probe_re, probe_im, frames_hbm, tab_hbm,
    new_re, new_im,
    po, acc, light, term, amp, wave, turns, frames, tab, probe, swaps, base,
    side_out, side_in, corner_out, corner_in,
    lrow_in, lside_out, lside_in, lcorner_out, lcorner_in,
    grow_in, gside_out, gside_in, gcorner_out, gcorner_in,
    count_ref, off_ref, idx_ref, newv, local_sem, send_sem, recv_sem, out_sem,
):
    row, col = lax.axis_index("row"), lax.axis_index("col")
    n_row, n_col = lax.axis_size("row"), lax.axis_size("col")
    peers = [(row + dr, col + dc) for dr, dc in SIDES]
    there = []
    for dr, dc in SIDES:
        ok = []
        if dr:
            ok.append(row > 0 if dr < 0 else row < n_row - 1)
        if dc:
            ok.append(col > 0 if dc < 0 else col < n_col - 1)
        there.append(ok[0] if len(ok) == 1 else ok[0] & ok[1])

    barrier = pltpu.get_barrier_semaphore()
    for k in range(8):
        @pl.when(there[k])
        def _():
            pl.semaphore_signal(barrier, inc=1, device_id=peers[k], device_id_type=pl.DeviceIdType.MESH)

    loads = []
    for b in (0, 3, 1, 2):
        for i, source in enumerate((obj_re, obj_im)):
            loads.append((source.at[:, :, pl.ds(128 * b, 128)], po.at[i, b + 1, 2:26]))
    loads += [(probe_re, probe.at[0]), (probe_im, probe.at[1]), (frames_hbm, frames), (tab_hbm, tab)]
    loads += [(count_hbm, count_ref), (off_hbm, off_ref), (idx_hbm, idx_ref)]
    loads = [pltpu.make_async_copy(s, d, local_sem.at[i]) for i, (s, d) in enumerate(loads)]
    for load in loads:
        load.start()

    def message(phase, k, source, target):
        return pltpu.make_async_remote_copy(
            src_ref=source,
            dst_ref=target,
            send_sem=send_sem.at[phase, k],
            recv_sem=recv_sem.at[phase, BACK[k]],
            device_id=peers[k],
            device_id_type=pl.DeviceIdType.MESH,
        )

    def messages(phase, rows_of, side_o, side_i, corner_o, corner_i):
        out = []
        for k, (dr, dc) in enumerate(SIDES):
            j = BACK[k]
            if dc == 0:
                out.append(message(phase, k, *rows_of(k)))
            elif dr == 0:
                out.append(message(phase, k, side_o.at[k - 2], side_i.at[j - 2]))
            else:
                out.append(message(phase, k, corner_o.at[k - 4], corner_i.at[j - 4]))
        return out

    def start(group, some=(4, 5, 6, 7, 0, 1, 2, 3)):
        for k in some:
            @pl.when(there[k])
            def _():
                group[k].start()

    def arrive(group):
        for k in range(8):
            @pl.when(there[k])
            def _():
                group[BACK[k]].wait_recv()

    def drain(group):
        for k in range(8):
            @pl.when(there[k])
            def _():
                group[k].wait_send()

    def object_rows(k):
        if k == 0:
            return po.at[:, 1:5, 2:4], po.at[:, 1:5, 26:28]
        return po.at[:, 1:5, 24:26], po.at[:, 1:5, 0:2]

    def spilled_rows(ref, into):
        def rows_of(k):
            at = 0 if k == 0 else HALO + TR
            return ref.at[:, 0:4, at : at + HALO, :], into.at[1 - k]
        return rows_of

    objects = messages(0, object_rows, side_out, side_in, corner_out, corner_in)
    lights = messages(1, spilled_rows(light, lrow_in), lside_out, lside_in, lcorner_out, lcorner_in)
    grads = messages(2, spilled_rows(acc, grow_in), gside_out, gside_in, gcorner_out, gcorner_in)

    for load in loads[:4]:
        load.wait()
    for i in range(2):
        side_out[0, i] = pack(po[i, 1, 2:26].reshape(TR, 128), False)
        side_out[1, i] = pack(po[i, 4, 2:26].reshape(TR, 128), True)
        for k in range(4, 8):
            dr, dc = SIDES[k]
            at = 2 if dr < 0 else 24
            corner_out[k - 4, i] = pack(po[i, 1 if dc < 0 else 4, at : at + 2].reshape(HALO, 128), dc > 0)

    for load in loads[4:8]:
        load.wait()
    neighbours = sum(t.astype(jnp.int32) for t in there)
    pl.semaphore_wait(barrier, neighbours)
    start(objects)

    for k, (dr, dc) in enumerate(SIDES):
        @pl.when(jnp.logical_not(there[k]))
        def _():
            if dc == 0:
                at = 0 if dr < 0 else 26
                po[:, 1:5, at : at + 2] = jnp.zeros((2, 4, 2, 16, 128), F32)
                h = 0 if dr < 0 else 1
                lrow_in[h] = jnp.zeros((1, 4, HALO, 128), F32)
                grow_in[h] = jnp.zeros((2, 4, HALO, 128), F32)
            elif dr == 0:
                for ref in (side_in, lside_in, gside_in):
                    ref[k - 2] = jnp.zeros(ref.shape[1:], F32)
            else:
                for ref in (corner_in, lcorner_in, gcorner_in):
                    ref[k - 4] = jnp.zeros(ref.shape[1:], F32)

    def clear(j, _):
        for i in range(2):
            term[i, pl.ds(40 * j, 12)] = jnp.zeros((12, 16, 128), F32)
            term[i, pl.ds(40 * j + 28, 12)] = jnp.zeros((12, 16, 128), F32)
        return 0

    lax.fori_loop(0, 3 * SLOTS + 1, clear, 0)
    for i in range(2):
        term[i, 120 * SLOTS + 12 : 120 * SLOTS + 28] = jnp.zeros((16, 16, 128), F32)
    swaps[0], swaps[1] = orders()

    for load in loads[8:]:
        load.wait()
    for i in range(2):
        for h in range(2):
            for k in range(8):
                turns[k, i, h] = turned(probe[i, :, 128 * h : 128 * h + 128], 16 * k)
    count = count_ref[0, 0]

    def unit(x):
        return lax.max(lax.min(x, 1), 0)

    def place(s):
        p = lax.div(off_ref[0, s] + HALO, 16)
        c = off_ref[1, s] + 128
        return p, lax.div(c, 128), lax.rem(c, 128)

    for s in range(SLOTS):
        p, q, _ = place(s)
        for b in range(6):
            j = b - q
            inside = unit(j + 1) * unit(3 - j) * unit(count - s)
            block = 3 * SLOTS + inside * (3 * s + j - 3 * SLOTS)
            base[6 * s + b] = 40 * block + 12 - p

    def total(i, b, at, groups):
        out = None
        for s in range(SLOTS):
            piece = term[i, pl.ds(base[6 * s + b] + at, groups)]
            out = piece if out is None else out + piece
        return out.reshape(16 * groups, 128)

    def spill_rows(into, i):
        for b in range(4):
            for at in (0, 26):
                into[i, b, 16 * at : 16 * at + 32, :] = total(i, b + 1, at, 2)

    def spill_edge(into, i):
        def edge(g, _):
            both = jnp.where(lanes(64) < 64, total(i, 5, 4 * g, 4), total(i, 0, 4 * g, 4))
            into[i, 4, pl.ds(pl.multiple_of(64 * g, 64), 64), :] = both
            return 0

        lax.fori_loop(0, 7, edge, 0)

    def inner(into, i):
        def rows(g, _):
            for b in range(4):
                into[i, b, pl.ds(pl.multiple_of(HALO + 64 * g, 32), 64), :] = total(i, b + 1, 2 + 4 * g, 4)
            return 0

        lax.fori_loop(0, 6, rows, 0)

    def keep(s, i, r, at, h, value):
        def at_block(j):
            return pl.ds(120 * s + (40 * j + 12 + at // 16), value.shape[0] // 16)

        shape = (value.shape[0] // 16, 16, 128)
        if h == 1:
            term[i, at_block(1)] = value.reshape(shape)
            return
        mine = lanes(value.shape[0]) >= r
        term[i, at_block(0)] = jnp.where(mine, value, 0.0).reshape(shape)
        term[i, at_block(2)] = jnp.where(mine, 0.0, value).reshape(shape)

    def prepare(s, _):
        _, _, r = place(s)
        mixed = dot(frames[idx_ref[0, s]], swaps[0]).astype(BF16)
        amp[s] = jnp.sqrt(dot(swaps[1], mixed))
        by = lax.div(r, 16)
        for at in range(0, PS, ROWS):
            rows = slice(at, at + ROWS)
            other = lanes(ROWS) < r
            kept = []
            for i in range(2):
                a, b = (turns[by, i, h, rows, :] for h in (0, 1))
                kept.append((jnp.where(other, b, a), jnp.where(other, a, b)))
                for h in range(2):
                    wave[s, i, h, rows, :] = kept[i][h]
            for h in range(2):
                keep(s, 0, r, at, h, kept[0][h] * kept[0][h] + kept[1][h] * kept[1][h])
        return 0

    lax.fori_loop(0, SLOTS, prepare, 0)
    spill_rows(light, 0)
    spill_edge(light, 0)
    inner(light, 0)

    def pack_spill(ref, side_o, corner_o):
        for i in range(ref.shape[0]):
            for h in range(2):
                side_o[h, i] = pack(ref[i, 4, HALO : HALO + TR, :], h == 0)
            for k in range(4, 8):
                dr, dc = SIDES[k]
                at = 0 if dr < 0 else HALO + TR
                corner_o[k - 4, i] = pack(ref[i, 4, at : at + HALO, :], dc < 0)

    pack_spill(light, lside_out, lcorner_out)

    arrive(objects)
    for i in range(2):
        for at, rows, low, high in (
            (0, HALO, corner_in[1, i], corner_in[0, i]),
            (HALO, TR, side_in[1, i], side_in[0, i]),
            (HALO + TR, HALO, corner_in[3, i], corner_in[2, i]),
        ):
            for b, side in ((5, unpack(low, False)), (0, unpack(high, True))):
                po[i, b, at // 16 : (at + rows) // 16] = side.reshape(rows // 16, 16, 128)
    start(lights)

    def slot(s):
        p, q, r = place(s)

        def patch():
            out = []
            for i in range(2):
                first, middle, last = (po[i, q + j, pl.ds(p, 16)].reshape(PS, 128) for j in range(3))
                out.append((jnp.where(lanes(PS) >= r, first, last), middle))
            return out

        return slot_terms(
            patch,
            lambda: [[wave[s, i, h] for h in range(2)] for i in range(2)],
            lambda: (amp[s, 0:128], amp[s, 128:256]),
            tab,
            lambda i, h, value: keep(s, i, r, 0, h, value),
        )

    def step(j, _):
        first, second = slot(2 * j), slot(2 * j + 1)
        next(first)
        for _ in range(8):
            next(second)
            next(first)
        next(second)
        return 0

    lax.fori_loop(0, SLOTS // 2, step, 0)
    for i in range(2):
        spill_rows(acc, i)
    start(grads, (0, 1))
    for i in range(2):
        spill_edge(acc, i)
    pack_spill(acc, gside_out, gcorner_out)
    start(grads, (4, 5, 6, 7, 2, 3))
    for i in range(2):
        inner(acc, i)

    def absorb(ref, row_in, side_i, corner_i):
        for i in range(ref.shape[0]):
            for h, at in ((0, HALO), (1, TR)):
                ref[i, 0:4, at : at + HALO, :] += row_in[h, i]
            for h, b in ((0, 0), (1, 3)):
                keep = lanes(TR) < 32 if h == 0 else lanes(TR) >= 96
                ref[i, b, HALO : HALO + TR, :] += jnp.where(keep, unpack(side_i[h, i], h == 1), 0.0)
            for k in range(4, 8):
                dr, dc = SIDES[k]
                at = HALO if dr < 0 else TR
                keep = lanes(HALO) < 32 if dc < 0 else lanes(HALO) >= 96
                ref[i, 0 if dc < 0 else 3, at : at + HALO, :] += jnp.where(keep, unpack(corner_i[k - 4, i], dc > 0), 0.0)

    arrive(lights)
    absorb(light, lrow_in, lside_in, lcorner_in)
    for b in range(4):
        light[0, b, HALO : HALO + TR, :] = 1.0 / (light[0, b, HALO : HALO + TR, :] + 1.0)
    rows = pl.ds(HALO, TR)
    outs = (new_re, new_im)
    for i in range(2):
        for b in range(4):
            mine = po[i, b + 1, 2:26].reshape(TR, 128) - acc[i, b, rows, :] * light[0, b, rows, :]
            newv[i, :, 128 * b : 128 * b + 128] = mine

    def leave(i, j, down, across):
        return pltpu.make_async_copy(newv.at[i, down, across], outs[i].at[down, across], out_sem.at[i, j])

    middle = pl.ds(HALO, TR - 2 * HALO)
    first = [leave(i, 0, middle, pl.ds(128, 256)) for i in range(2)]
    last = []
    for i in range(2):
        last += [leave(i, 1, pl.ds(0, HALO), pl.ds(0, TC)), leave(i, 2, pl.ds(TR - HALO, HALO), pl.ds(0, TC))]
        last += [leave(i, 3, middle, pl.ds(0, 128)), leave(i, 4, middle, pl.ds(384, 128))]
    for copy in first:
        copy.start()
    arrive(grads)
    for i in range(2):
        for h, at in ((0, 0), (1, TR - HALO)):
            for b in range(4):
                newv[i, at : at + HALO, 128 * b : 128 * b + 128] -= grow_in[h, i, b] * light[0, b, HALO + at : 2 * HALO + at, :]
        for h, b in ((0, 0), (1, 3)):
            across = slice(128 * b, 128 * b + 128)
            part = unpack(gside_in[h, i], h == 1)
            ends = [unpack(gcorner_in[2 * v + h, i], h == 1) for v in range(2)]
            low = jnp.concatenate([part[:HALO] + ends[0], part[HALO : TR - HALO], part[TR - HALO :] + ends[1]], 0)
            keep_lanes = lanes(TR) < 32 if h == 0 else lanes(TR) >= 96
            newv[i, :, across] -= jnp.where(keep_lanes, low * light[0, b, rows, :], 0.0)
    for copy in last:
        copy.start()
    for copy in first + last:
        copy.wait()
    for group in (objects, lights, grads):
        drain(group)


def write_out(re, im, new_re, new_im, held, sem):
    into, out = [], []
    for i, (source, target) in enumerate(((re, new_re), (im, new_im))):
        for j in range(8):
            rows = pl.ds(48 * j, 48)
            into.append(pltpu.make_async_copy(source.at[rows], held.at[i, rows], sem.at[0, i, j]))
            out.append(pltpu.make_async_copy(held.at[i, rows], target.at[rows], sem.at[1, i, j]))
    for copy in into:
        copy.start()
    for before, after in zip(into, out):
        before.wait()
        after.start()
    for copy in out:
        copy.wait()


def shards(object_re, object_im, probe_re, probe_im, frames, counts, offsets, frame_index):
    anywhere = pl.BlockSpec(memory_space=pl.ANY)
    spills = []
    for n in (1, 2):
        spills += [
            pltpu.VMEM((2, n, 4, HALO, 128), F32),
            pltpu.VMEM((2, n, 96, 128), F32),
            pltpu.VMEM((2, n, 96, 128), F32),
            pltpu.VMEM((4, n, 8, 128), F32),
            pltpu.VMEM((4, n, 8, 128), F32),
        ]
    results = pl.pallas_call(
        kernel,
        out_shape=(jax.ShapeDtypeStruct((TR, TC), F32),) * 2,
        in_specs=[anywhere] * 9,
        out_specs=(anywhere, anywhere),
        scratch_shapes=[
            pltpu.VMEM((2, 6, 28, 16, 128), F32),
            pltpu.VMEM((2, 5, WIDE, 128), F32),
            pltpu.VMEM((1, 5, WIDE, 128), F32),
            pltpu.VMEM((2, 40 * (3 * SLOTS + 1), 16, 128), F32),
            pltpu.VMEM((SLOTS, PS, PS), F32),
            pltpu.VMEM((SLOTS, 2, 2, PS, 128), F32),
            pltpu.VMEM((8, 2, 2, PS, 128), F32),
            pltpu.VMEM((8, PS, PS), BF16),
            pltpu.VMEM((4, 2, PS, PS), BF16),
            pltpu.VMEM((2, PS, PS), F32),
            pltpu.VMEM((2, PS, PS), BF16),
            pltpu.SMEM((6 * SLOTS,), jnp.int32),
            pltpu.VMEM((2, 2, 96, 128), F32),
            pltpu.VMEM((2, 2, 96, 128), F32),
            pltpu.VMEM((4, 2, 8, 128), F32),
            pltpu.VMEM((4, 2, 8, 128), F32),
            *spills,
            pltpu.SMEM((1, 1), jnp.int32),
            pltpu.SMEM((2, SLOTS), jnp.int32),
            pltpu.SMEM((1, SLOTS), jnp.int32),
            pltpu.VMEM((2, TR, TC), F32),
            pltpu.SemaphoreType.DMA((15,)),
            pltpu.SemaphoreType.DMA((3, 8)),
            pltpu.SemaphoreType.DMA((3, 8)),
            pltpu.SemaphoreType.DMA((2, 5)),
        ],
        compiler_params=pltpu.CompilerParams(
            collective_id=0, has_side_effects=True, vmem_limit_bytes=63 << 20
        ),
    )(
        counts, offsets[0, 0].T, frame_index.reshape(1, SLOTS),
        object_re.reshape(24, 16, TC), object_im.reshape(24, 16, TC), probe_re, probe_im, frames.reshape(8, PS, PS), jnp.asarray(tables()),
    )
    return pl.pallas_call(
        write_out,
        out_shape=(jax.ShapeDtypeStruct((TR, TC), F32),) * 2,
        in_specs=[anywhere] * 2,
        out_specs=(anywhere,) * 2,
        scratch_shapes=[pltpu.VMEM((2, TR, TC), F32), pltpu.SemaphoreType.DMA((2, 2, 8))],
        compiler_params=pltpu.CompilerParams(vmem_limit_bytes=63 << 20),
    )(*results)


def solution(mesh):
    return jax.shard_map(
        shards,
        mesh=mesh,
        in_specs=(
            P("row", "col"),
            P("row", "col"),
            P(),
            P(),
            P("row", "col", None, None, None),
            P("row", "col"),
            P("row", "col", None, None),
            P("row", "col", None),
        ),
        out_specs=(P("row", "col"), P("row", "col")),
        check_vma=False,
    )
```
